32 devices in a mesh: expert: 8 (over z, y), tensor: 4 (over x, core).
Axes of the slice: x: 2, y: 2, z: 4, core: 2. Of those that a mesh axis runs over, the one named last changes fastest.
Arguments:
- tokens: bfloat16 [3152, 1024], P('expert'), may hold values from -6 to 6
- gain_attn: float32 [1024], replicated, may hold values from 0.5 to 1.5
- shift_attn: float32 [1024], replicated, may hold values from -1.75 to 1.75
- w_qkv: bfloat16 [3, 1024, 1024], P(None, None, 'tensor'), may hold values from -0.1875 to 0.1875
- b_qv: float32 [2, 1024], P(None, 'tensor'), may hold values from -1.75 to 1.75
- w_out: bfloat16 [1024, 1024], P('tensor'), may hold values from -2 to 2
- b_out: float32 [1024], replicated, may hold values from -1.75 to 1.75
- gain_moe: float32 [1024], replicated, may hold values from 0.5 to 1.5
- shift_moe: float32 [1024], replicated, may hold values from -1.75 to 1.75
- w_router: bfloat16 [1024, 8], replicated, may hold values from -0.125 to 0.125
- w_in: bfloat16 [8, 1024, 4096], P('expert', None, 'tensor'), may hold values from -0.1875 to 0.1875
- b_in: float32 [8, 4096], P('expert', 'tensor'), may hold values from -1.75 to 1.75
- w_back: bfloat16 [8, 4096, 1024], P('expert', 'tensor'), may hold values from -0.625 to 0.625
- b_back: float32 [8, 1024], P('expert'), may hold values from -5 to 5
- routes: int32 [3152, 2], P('expert'), may hold values from 0 to 7, all different within a row; in each aligned block of 394 rows (0 to 393, 394 to 787, ...) at most 160 rows name the same one
- d_out: bfloat16 [3152, 1024], P('expert'), may hold values from -8 to 8
Outputs:
- activations: bfloat16 [3152, 1024], P('expert')
- d_tokens: float32 [3152, 1024], P('expert')
- d_gain_attn: float32 [1024], replicated
- d_shift_attn: float32 [1024], replicated
- d_w_qkv: float32 [3, 1024, 1024], P(None, None, 'tensor')
- d_b_qv: float32 [2, 1024], P(None, 'tensor')
- d_w_out: float32 [1024, 1024], P('tensor')
- d_b_out: float32 [1024], replicated
- d_gain_moe: float32 [1024], replicated
- d_shift_moe: float32 [1024], replicated
- d_w_router: float32 [1024, 8], replicated
- d_w_in: float32 [8, 1024, 4096], P('expert', None, 'tensor')
- d_b_in: float32 [8, 4096], P('expert', 'tensor')
- d_w_back: float32 [8, 4096, 1024], P('expert', 'tensor')
- d_b_back: float32 [8, 1024], P('expert')
The draws below stay inside these ranges and needn't reach their ends.
Inputs may be any that keep to these rules, and one draw needn't show every extreme that they name: `routes`: in the rows of one device no expert is named more than 160 times, and a token's 2 choices differ.
All inputs are finite; a program needn't handle non-finite values.
Results may differ from the reference program's by a relative error of at most 0.019.
Values may be sent and summed in bfloat16 or wider, within the bound.
No kernel may reach another device: no remote copies, remote signals or barrier semaphores. Data moves between devices by JAX's collectives and lax.ppermute only.
A program may use at most 128 MiB of HBM per device.

```python
import math
from functools import partial
import jax
import jax.numpy as jnp
import numpy as np
from jax import lax

D = 1024
H = 16
HD = 64
FF = 4096
TOP = 2
SEQ = 197
IMG_DEV = 2
TOK_DEV = 394
EXPERTS = 8
TOKENS = 3152
CAP = 160
N_EXPERT = 8


def draw_d_out(key, part):
    row_frac = jnp.arange(TOKENS, dtype=jnp.float32)[:, None] / TOKENS
    row_scale = 0.6 * jnp.exp(row_frac * jnp.log(3.0))
    base_draw = jnp.clip(jax.random.normal(key, (TOKENS, D), jnp.float32), -4.0, 4.0)
    return (base_draw * row_scale).astype(jnp.bfloat16)


def block_levels(key, extent, shards, smallest, high):
    gain = 1.0
    for dim, shards_of in shards:
        heights = jax.random.uniform(jax.random.fold_in(jax.random.fold_in(key, 6), dim), (shards_of,), jnp.float32, smallest / len(shards), high / len(shards))
        gain = gain * jnp.repeat(jnp.exp(heights), extent[dim] // shards_of).reshape((-1,) + (1,) * (len(extent) - 1 - dim))
    return gain


def routed_block(own_key, own, number, rows, amount, top, most, skew):
    sequence = jax.random.permutation(own_key, amount)
    packed, usual = load_shares(amount, rows * top, most, skew, True), load_shares(amount, rows * top, most, skew, False)
    places = jnp.arange(amount)

    def named(tallies, rotation):
        used = int((tallies > 0).sum())
        fixed = max(1, used // 4)
        passed = fixed + (places - fixed + rotation * (used - fixed)) % max(1, amount - fixed)
        return jnp.zeros((amount,), jnp.int32).at[sequence[jnp.where(places < fixed, places, passed)]].set(jnp.asarray(tallies, jnp.int32))

    tallies = jnp.where(number % 4 == 0, named(packed, number // 4), named(usual, number - number // 4 - 1))
    mixed = jax.random.permutation(jax.random.fold_in(own, 3), amount)
    donor, receiver = mixed[0:amount // 2 * 2:2], mixed[1:amount // 2 * 2:2]
    room = jnp.minimum(tallies[donor] - 1, most - tallies[receiver]) // 2
    room = jnp.where((donor == sequence[0]) | (receiver == sequence[0]) | (tallies[receiver] == 0), 0, jnp.maximum(room, 0))
    passed = jax.random.randint(jax.random.fold_in(own, 4), (amount // 2,), 0, 1 << 20) % (room + 1)
    tallies = tallies.at[donor].add(-passed).at[receiver].add(passed)
    labels = jnp.searchsorted(jnp.cumsum(tallies), jnp.arange(rows * top), side="right").astype(jnp.int32)
    table = labels.reshape(top, rows).T
    table = table[jax.random.permutation(jax.random.fold_in(own, 1), rows)]
    rotation = jax.random.randint(jax.random.fold_in(own, 2), (rows, 1), 0, top)
    return jnp.take_along_axis(table, (jnp.arange(top)[None, :] + rotation) % top, axis=1)


def load_shares(amount, total, limit, skew, full):
    portions = [(1 << 20) // math.isqrt(standing ** skew) + 1 for standing in range(1, amount + 1)]
    largest = limit if full else min(limit, max(-(-total // amount), total * portions[0] // sum(portions)))
    least = 1 if total - largest >= amount - 1 else 0
    holding, rest = [largest] + [least] * (amount - 1), total - largest - least * (amount - 1)
    while rest > 0:
        free = [i for i in range(1, amount) if holding[i] < largest] or [i for i in range(1, amount) if holding[i] < limit]
        whole, budget = sum([portions[i] for i in free]), rest
        for i in free:
            addition = min(limit - holding[i], max(1, budget * portions[i] // whole), rest)
            holding[i] = holding[i] + addition
            rest = rest - addition
    return np.array(holding)


def centred(rng, shape, scale, limit, pieces=(), held_as=jnp.bfloat16):
    loudness = block_levels(rng, shape, pieces, -0.22, 0.18) if pieces else 1.0
    entries = jax.random.normal(rng, shape, jnp.float32) * scale * loudness
    return jnp.minimum(jnp.maximum(entries, -limit), limit).astype(held_as)


def setup_inputs(seed: int = 0) -> dict:
    keys = jax.random.split(jax.random.key(seed), 17)
    tokens = centred(keys[0], (TOKENS, D), 1.0, 6.0, ((0, 8),))
    gain_attn = jnp.clip(1.0 + 0.1 * jax.random.normal(keys[1], (D,), jnp.float32), 0.5, 1.5)
    shift_attn = centred(keys[2], (D,), 0.3, 1.75, (), jnp.float32)
    w_qkv = centred(keys[3], (3, D, H * HD), D ** -0.5, 0.1875, ((2, 4),))
    b_qv = centred(keys[4], (2, H * HD), 0.3, 1.75, ((1, 4),), jnp.float32)
    w_out = centred(keys[5], (H * HD, D), (max(1, H * HD // 128)) ** -0.5, 2.0, ((0, 4),))
    b_out = centred(keys[6], (D,), 0.3, 1.75, (), jnp.float32)
    gain_moe = jnp.clip(1.0 + 0.1 * jax.random.normal(keys[7], (D,), jnp.float32), 0.5, 1.5)
    shift_moe = centred(keys[8], (D,), 0.3, 1.75, (), jnp.float32)
    w_router = centred(keys[9], (D, EXPERTS), (2 * D) ** -0.5, 0.125)
    w_in = centred(keys[10], (EXPERTS, D, FF), D ** -0.5, 0.1875, ((0, 8), (2, 4)))
    b_in = centred(keys[11], (EXPERTS, FF), 0.3, 1.75, ((0, 8), (1, 4)), jnp.float32)
    w_back = centred(keys[12], (EXPERTS, FF, D), (max(1, FF * 3 // (2 * EXPERTS * EXPERTS))) ** -0.5, 0.625, ((0, 8), (1, 4)))
    b_back = centred(keys[13], (EXPERTS, D), (EXPERTS / 10), 5.0, ((0, 8),), jnp.float32)
    routes_keys = jax.random.split(jax.random.fold_in(keys[14], 1), TOKENS // TOK_DEV)
    routes_turns = jax.random.permutation(jax.random.fold_in(keys[14], 3), TOKENS // TOK_DEV)
    routes = jax.vmap(lambda own, number: routed_block(jax.random.fold_in(keys[14], 2), own, number, TOK_DEV, EXPERTS, TOP, CAP, 2))(routes_keys, routes_turns).reshape((TOKENS, TOP))
    d_out = draw_d_out(jax.random.fold_in(keys[16], 71), 0)
    return {"tokens": tokens, "gain_attn": gain_attn, "shift_attn": shift_attn, "w_qkv": w_qkv, "b_qv": b_qv, "w_out": w_out, "b_out": b_out, "gain_moe": gain_moe, "shift_moe": shift_moe, "w_router": w_router, "w_in": w_in, "b_in": b_in, "w_back": w_back, "b_back": b_back, "routes": routes, "d_out": d_out}


@jax.custom_vjp
def low(v):
    return lax.optimization_barrier(v.astype(jnp.bfloat16)).astype(jnp.float32)

@jax.custom_vjp
def low_back(v):
    return v

def low_keep(v):
    return (low(v), None)

def low_pass(kept, grad):
    return (grad,)

def back_keep(v):
    return (v, None)

def back_low(kept, grad):
    return (low(grad),)
low.defvjp(low_keep, low_pass)
low_back.defvjp(back_keep, back_low)
precise = lax.Precision.HIGHEST
epsilon = 1e-06

def layer_norm(values, gain_vec, shift_vec):
    center = values - lax.optimization_barrier(jnp.mean(values, axis=-1, keepdims=True))
    variance = lax.optimization_barrier(jnp.mean(center * center, axis=-1, keepdims=True))
    return center * lax.rsqrt(variance + epsilon) * gain_vec + shift_vec

def attend(device_rows, w_qkv, b_qv):
    project = jnp.einsum('td,sdf->stf', device_rows, w_qkv, precision=precise)
    queries = low(low_back(project[0] + b_qv[0]))
    key_rows = low(low_back(project[1]))
    value_rows = low(low_back(project[2] + b_qv[1]))
    head_shape = (IMG_DEV, SEQ, H, HD)
    scores = jnp.einsum('iqhc,ikhc->ihqk', queries.reshape(head_shape), key_rows.reshape(head_shape), precision=precise)
    scores = low_back(scores * HD ** (-0.5))
    attn_probs = jax.nn.softmax(scores, axis=-1)
    mixed_heads = jnp.einsum('ihqk,ikhc->iqhc', low(attn_probs), value_rows.reshape(head_shape), precision=precise)
    return low(low_back(mixed_heads.reshape(TOK_DEV, H * HD)))

def slot_table(route_rows):
    onehot_int = (route_rows[:, None] == jnp.arange(EXPERTS, dtype=jnp.int32)[None, :]).astype(jnp.int32)
    earlier = jnp.cumsum(onehot_int, axis=0) - onehot_int
    return (route_rows * CAP + lax.optimization_barrier(jnp.sum(earlier * onehot_int, axis=1))).astype(jnp.int32)

def run_expert(operands):
    rows_in, weight_in, bias_in, weight_back, bias_back = operands
    pre_act = low_back(jnp.dot(rows_in, weight_in, precision=precise) + bias_in)
    activated = low(jax.nn.gelu(pre_act, approximate=False))
    return low_back(jnp.dot(activated, weight_back, precision=precise) + bias_back)

def forward(tokens, gain_attn, shift_attn, w_qkv, b_qv, w_out, b_out, gain_moe, shift_moe, w_router, w_in, b_in, w_back, b_back, routes):
    normed = low(layer_norm(tokens, gain_attn, shift_attn))

    def attend_block(device_rows):
        return attend(device_rows, w_qkv, b_qv)
    mixed_heads = lax.map(jax.checkpoint(attend_block), normed.reshape(N_EXPERT, TOK_DEV, D))
    mixed_heads = mixed_heads.reshape(TOKENS, H * HD)
    branch = low_back(jnp.dot(mixed_heads, w_out, precision=precise)) + b_out
    residual = tokens + branch
    second_low = low(layer_norm(residual, gain_moe, shift_moe))
    logits = low_back(jnp.dot(second_low, w_router, precision=precise))
    router_probs = jax.nn.softmax(logits, axis=-1)
    gate_vals = jnp.take_along_axis(router_probs, routes, axis=1)
    route_rows = routes.reshape(N_EXPERT, TOK_DEV * TOP)
    targets = jax.vmap(slot_table)(route_rows)
    sources = jnp.broadcast_to(jnp.arange(N_EXPERT, dtype=jnp.int32)[:, None], targets.shape)
    sent_rows = jnp.repeat(second_low.reshape(N_EXPERT, TOK_DEV, D), TOP, axis=1)
    buffers = jnp.zeros((N_EXPERT, EXPERTS * CAP, D), jnp.float32).at[sources, targets].add(sent_rows)
    by_expert = buffers.reshape(N_EXPERT, EXPERTS, CAP, D).transpose(1, 0, 2, 3).reshape(EXPERTS, N_EXPERT * CAP, D)
    results = lax.map(jax.checkpoint(run_expert), (by_expert, w_in, b_in, w_back, b_back))
    results = results.reshape(EXPERTS, N_EXPERT, CAP, D).transpose(1, 0, 2, 3).reshape(N_EXPERT, EXPERTS * CAP, D)
    picked = results[sources, targets].reshape(TOKENS, TOP, D)
    mixture = lax.optimization_barrier(jnp.sum(gate_vals[:, :, None] * picked, axis=1))
    return residual + mixture

def reference(tokens, gain_attn, shift_attn, w_qkv, b_qv, w_out, b_out, gain_moe, shift_moe, w_router, w_in, b_in, w_back, b_back, routes, d_out):
    floats = (tokens.astype(jnp.float32), gain_attn, shift_attn, w_qkv.astype(jnp.float32), b_qv, w_out.astype(jnp.float32), b_out, gain_moe, shift_moe, w_router.astype(jnp.float32), w_in.astype(jnp.float32), b_in, w_back.astype(jnp.float32), b_back)
    outputs, pullback = jax.vjp(partial(forward, routes=routes), *floats)
    gradients = pullback(d_out.astype(jnp.float32))
    return (outputs.astype(jnp.bfloat16), gradients[0], gradients[1], gradients[2], gradients[3], gradients[4], gradients[5], gradients[6], gradients[7], gradients[8], gradients[9], gradients[10], gradients[11], gradients[12], gradients[13])
```

```python
import functools

import jax
import jax.numpy as jnp
from jax import lax
from jax.experimental import pallas as pl
from jax.experimental.pallas import tpu as pltpu
from jax.sharding import PartitionSpec as P

HD = 64
SEQ = 197
LANES = 128
VMEM_LIMIT = 52 * 1024 * 1024

epsilon = 1e-06
f32 = jnp.float32
bf16 = jnp.bfloat16


def dot(left, right, left_dim, right_dim, precision=None):
    return lax.dot_general(
        left,
        right,
        (((left_dim,), (right_dim,)), ((), ())),
        precision=precision,
        preferred_element_type=f32,
    )


def call(body, outs, ins, flops, grid=None, in_specs=None, out_specs=None, scalars=0):
    specs = {}
    if grid is not None:
        specs["grid"] = grid
        specs["in_specs"] = in_specs
        specs["out_specs"] = out_specs
    else:
        specs["in_specs"] = [
            pl.BlockSpec(memory_space=pltpu.SMEM if i < scalars else pltpu.VMEM)
            for i in range(len(ins))
        ]
        specs["out_specs"] = [pl.BlockSpec(memory_space=pltpu.VMEM) for _ in outs]
    moved = sum(a.size * a.dtype.itemsize for a in list(ins) + list(outs))
    return pl.pallas_call(
        body,
        out_shape=outs,
        compiler_params=pltpu.CompilerParams(vmem_limit_bytes=VMEM_LIMIT),
        cost_estimate=pl.CostEstimate(flops=flops, bytes_accessed=moved, transcendentals=0),
        **specs,
    )(*ins)


def sds(shape, dtype):
    return jax.ShapeDtypeStruct(shape, dtype)


def swap(values, axis, bit):
    count = lax.axis_size(axis)
    return lax.ppermute(values, axis, [(i, i ^ bit) for i in range(count)])


def bits_of(count):
    return [1 << i for i in range(count.bit_length() - 1)]


def gather_tensor(values):
    count = lax.axis_size("tensor")
    blocks = {0: values}
    for bit in reversed(bits_of(count)):
        for key in list(blocks):
            blocks[key | bit] = swap(blocks[key], "tensor", bit)
    stacked = jnp.stack([blocks[key] for key in range(count)])
    order = lax.axis_index("tensor") ^ jnp.arange(count)
    return jnp.stack(
        [lax.dynamic_index_in_dim(stacked, order[key], 0, keepdims=False) for key in range(count)]
    )


def scatter_tensor(pieces):
    held = dict(enumerate(pieces))
    for bit in bits_of(len(pieces)):
        for key in sorted(held):
            if key & bit:
                came = swap(held.pop(key), "tensor", bit)
                mine = held[key ^ bit]
                held[key ^ bit] = (mine.astype(f32) + came.astype(f32)).astype(mine.dtype)
    return held[0]


def butterfly(values, axis):
    for bit in bits_of(lax.axis_size(axis)):
        came = swap(values, axis, bit)
        values = (values.astype(f32) + came.astype(f32)).astype(values.dtype)
    return values


def sum_experts(values, order):
    index = lax.axis_index("expert")
    for bit in order:
        half = values.shape[0] // 2
        side = (index & bit) // bit
        keep = lax.dynamic_slice_in_dim(values, side * half, half, 0)
        send = lax.dynamic_slice_in_dim(values, (1 - side) * half, half, 0)
        came = swap(send, "expert", bit)
        values = (keep.astype(f32) + came.astype(f32)).astype(bf16)
    for bit in reversed(order):
        side = (index & bit) // bit
        came = swap(values, "expert", bit)
        values = jnp.where(
            side == 0,
            jnp.concatenate([values, came], 0),
            jnp.concatenate([came, values], 0),
        )
    return values


def norm_parts(values):
    center = values - jnp.mean(values, axis=-1, keepdims=True)
    variance = jnp.mean(center * center, axis=-1, keepdims=True)
    rstd = lax.rsqrt(variance + epsilon)
    return center * rstd, rstd


def norm_back(grad, normal, rstd, gain):
    scaled = grad * gain
    mean_g = jnp.mean(scaled, axis=-1, keepdims=True)
    mean_gn = jnp.mean(scaled * normal, axis=-1, keepdims=True)
    return rstd * (scaled - mean_g - normal * mean_gn)


def same_image(rows):
    left = lax.broadcasted_iota(jnp.int32, (rows, rows), 0)
    right = lax.broadcasted_iota(jnp.int32, (rows, rows), 1)
    left_id = jnp.zeros((rows, rows), jnp.int32)
    right_id = jnp.zeros((rows, rows), jnp.int32)
    for edge in range(SEQ, rows, SEQ):
        left_id = left_id + (left >= edge).astype(jnp.int32)
        right_id = right_id + (right >= edge).astype(jnp.int32)
    return left_id == right_id


def head_probs(queries, keys, inside):
    scores = dot(queries, keys, 1, 1) * (HD ** (-0.5))
    scores = jnp.where(inside, scores, -1e30)
    top = jnp.max(scores, axis=-1, keepdims=True)
    powers = jnp.exp(scores - top)
    return powers * (1.0 / jnp.sum(powers, axis=-1, keepdims=True))


def lane_heads(rows):
    lane = lax.broadcasted_iota(jnp.int32, (rows, LANES), 1)
    return [(lane // HD) == head for head in range(LANES // HD)]


def attend_kernel(tok_ref, gain_ref, shift_ref, w_ref, b_ref, norm_ref, q_ref, k_ref, v_ref, mix_ref):
    rows = tok_ref.shape[0]
    normal, _ = norm_parts(tok_ref[...].astype(f32))
    normed = (normal * gain_ref[...] + shift_ref[...]).astype(bf16)
    norm_ref[...] = normed
    q_ref[...] = (dot(normed, w_ref[0], 1, 0) + b_ref[0:1, :]).astype(bf16)
    k_ref[...] = dot(normed, w_ref[1], 1, 0).astype(bf16)
    v_ref[...] = (dot(normed, w_ref[2], 1, 0) + b_ref[1:2, :]).astype(bf16)
    inside = same_image(rows)
    heads = lane_heads(rows)
    for start in range(0, q_ref.shape[1], LANES):
        cols = slice(start, start + LANES)
        queries, keys, value_rows = q_ref[:, cols], k_ref[:, cols], v_ref[:, cols]
        mixed = jnp.zeros((rows, LANES), f32)
        for mask in heads:
            probs = head_probs(jnp.where(mask, queries, 0).astype(bf16), keys, inside)
            mixed = jnp.where(mask, dot(probs.astype(bf16), value_rows, 1, 0), mixed)
        mix_ref[:, cols] = mixed.astype(bf16)


def route_kernel(idx_ref, routes_ref, dout_ref, place_ref, send_ref, *, experts, capacity):
    rows, slots = place_ref.shape
    width = send_ref.shape[1]
    routes = routes_ref[...]
    ids = lax.broadcasted_iota(jnp.int32, (rows, experts), 1)
    named = [routes[:, k : k + 1] == ids for k in range(routes.shape[1])]
    tally = sum(m.astype(f32) for m in named)
    above = lax.broadcasted_iota(jnp.int32, (rows, rows), 0)
    below = lax.broadcasted_iota(jnp.int32, (rows, rows), 1)
    earlier = dot((below < above).astype(f32).astype(bf16), tally.astype(bf16), 1, 0)
    base = earlier + (ids * capacity).astype(f32)
    slot_ids = lax.broadcasted_iota(jnp.int32, (rows, slots), 1)
    place = jnp.zeros((rows, slots), f32)
    for mask in named:
        target = jnp.sum(jnp.where(mask, base, 0.0), axis=1, keepdims=True).astype(jnp.int32)
        place = jnp.where(slot_ids == target, 1.0, place)
    place = place.astype(bf16)
    place_ref[...] = place
    start = pl.multiple_of(idx_ref[0] * width, LANES)
    send_ref[...] = dot(place, dout_ref[:, pl.ds(start, width)], 0, 0).astype(bf16)


def middle_kernel(
    idx_ref,
    mix_ref,
    w_ref,
    tok_ref,
    bias_ref,
    gain_ref,
    shift_ref,
    router_ref,
    place_ref,
    resid_ref,
    second_ref,
    probs_ref,
    send_ref,
):
    width = send_ref.shape[1]
    total = dot(mix_ref[0], w_ref[0], 1, 0)
    for block in range(1, mix_ref.shape[0]):
        total = total + dot(mix_ref[block], w_ref[block], 1, 0)
    residual = tok_ref[...].astype(f32) + total + bias_ref[...]
    resid_ref[...] = residual
    normal, _ = norm_parts(residual)
    second_ref[...] = (normal * gain_ref[...] + shift_ref[...]).astype(bf16)
    start = pl.multiple_of((idx_ref[0] & 1) * width, LANES)
    send_ref[...] = dot(place_ref[...], second_ref[:, pl.ds(start, width)], 0, 0).astype(bf16)
    logits = dot(second_ref[...], router_ref[...], 1, 0)
    powers = jnp.exp(logits - jnp.max(logits, axis=-1, keepdims=True))
    probs_ref[...] = powers / jnp.sum(powers, axis=-1, keepdims=True)


def expert_kernel(
    idx_ref,
    own_ref,
    other_ref,
    grad_ref,
    unscaled_ref,
    w_in_ref,
    b_in_ref,
    b_back_ref,
    router_ref,
    *outs,
    blocks,
):
    piece_refs = outs[:blocks]
    act_ref, pre_ref, grady_ref, gate_ref, gg_ref, dbin_ref, dbback_ref = outs[blocks:]
    tensor_id, expert_id = idx_ref[0], idx_ref[1]
    side = tensor_id & 1
    width = w_in_ref.shape[0] // 2
    piece = w_in_ref.shape[0] // blocks
    own, other = own_ref[...], other_ref[...]
    low_half = jnp.where(side == 0, own, other)
    high_half = jnp.where(side == 0, other, own)
    logits = dot(low_half, router_ref[0:width, :], 1, 0) + dot(
        high_half, router_ref[width:, :], 1, 0
    )
    powers = jnp.exp(logits - jnp.max(logits, axis=-1, keepdims=True))
    ids = lax.broadcasted_iota(jnp.int32, logits.shape, 1)
    gate = jnp.sum(jnp.where(ids == expert_id, powers, 0.0), axis=-1, keepdims=True) / jnp.sum(
        powers, axis=-1, keepdims=True
    )
    gate_ref[...] = gate
    pre_act = (
        dot(low_half, w_in_ref[0:width, :], 1, 0)
        + dot(high_half, w_in_ref[width:, :], 1, 0)
        + b_in_ref[...]
    )
    cdf = 0.5 * (1.0 + lax.erf(pre_act * (2.0**-0.5)))
    density = jnp.exp(-0.5 * pre_act * pre_act) * 0.3989422804014327
    act = (pre_act * cdf).astype(bf16)
    act_ref[...] = act
    unscaled = unscaled_ref[...]
    grad_pre = (gate * unscaled * (cdf + pre_act * density)).astype(bf16)
    pre_ref[...] = grad_pre
    grad_rows = grad_ref[...].astype(f32)
    gg_ref[...] = jnp.sum(act.astype(f32) * unscaled, axis=1, keepdims=True) + jnp.sum(
        grad_rows * b_back_ref[...], axis=1, keepdims=True
    ) * (1.0 / blocks)
    grad_y = (gate * grad_rows).astype(bf16)
    grady_ref[...] = grad_y

    @pl.when(pl.program_id(0) == 0)
    def _():
        dbin_ref[...] = jnp.zeros_like(dbin_ref)
        dbback_ref[...] = jnp.zeros_like(dbback_ref)

    dbin_ref[...] += jnp.sum(grad_pre.astype(f32), axis=0, keepdims=True)
    dbback_ref[...] += jnp.sum(grad_y.astype(f32), axis=0, keepdims=True)
    for key, piece_ref in enumerate(piece_refs):
        start = pl.multiple_of((tensor_id ^ key) * piece, LANES)
        piece_ref[...] = dot(grad_pre, w_in_ref[pl.ds(start, piece), :], 1, 1).astype(bf16)


def back_kernel(idx_ref, act_ref, gate_ref, w_ref, bias_ref, *piece_refs):
    blocks = len(piece_refs)
    piece = piece_refs[0].shape[1]
    for key, piece_ref in enumerate(piece_refs):
        cols = pl.ds(pl.multiple_of((idx_ref[0] ^ key) * piece, LANES), piece)
        rows = dot(act_ref[...], w_ref[:, cols], 1, 0) + bias_ref[:, cols] * (1.0 / blocks)
        piece_ref[...] = (gate_ref[...] * rows).astype(bf16)


def residual_kernel(
    disp_ref,
    gg_ref,
    place_ref,
    probs_ref,
    second_ref,
    router_ref,
    resid_ref,
    gain_ref,
    dout_ref,
    w_ref,
    mix_ref,
    grad_ref,
    dw_ref,
    gmix_ref,
    small_ref,
    *,
    capacity,
):
    probs = probs_ref[...]
    experts = probs.shape[1]
    slots = place_ref.shape[1]
    piece = disp_ref.shape[2]
    blocks = disp_ref.shape[0]
    owner = lax.broadcasted_iota(jnp.int32, (slots, experts), 0)
    first = lax.broadcasted_iota(jnp.int32, (slots, experts), 1) * capacity
    segment = ((owner >= first) & (owner < first + capacity)).astype(f32)
    grad_probs = dot(
        place_ref[...].astype(f32) * gg_ref[...], segment, 1, 0, lax.Precision.HIGHEST
    )
    grad_logits = (
        probs * (grad_probs - jnp.sum(probs * grad_probs, axis=1, keepdims=True))
    ).astype(bf16)
    second_grad = jnp.concatenate([disp_ref[b].astype(f32) for b in range(blocks)], axis=1)
    second_grad = second_grad + dot(grad_logits, router_ref[...], 1, 1)
    normal, rstd = norm_parts(resid_ref[...])
    grad_resid = dout_ref[...].astype(f32) + norm_back(second_grad, normal, rstd, gain_ref[...])
    grad_ref[...] = grad_resid
    branch = grad_resid.astype(bf16)
    gmix_ref[...] = dot(branch, w_ref[...], 1, 1).astype(bf16)
    dw_ref[...] = dot(mix_ref[...], branch, 0, 0).astype(bf16)
    small_ref[0:experts, :] = dot(grad_logits, second_ref[...], 0, 0)
    small_ref[experts : experts + 1, :] = jnp.sum(second_grad * normal, axis=0, keepdims=True)
    small_ref[experts + 1 : experts + 2, :] = jnp.sum(second_grad, axis=0, keepdims=True)
    small_ref[experts + 2 : experts + 3, :] = jnp.sum(grad_resid, axis=0, keepdims=True)


def attend_back_kernel(
    q_ref, k_ref, v_ref, gmix_ref, norm_ref, w_ref, dw_ref, db_ref, part_ref, gq_ref, gk_ref, gv_ref
):
    rows = q_ref.shape[0]
    inside = same_image(rows)
    heads = lane_heads(rows)
    scale = HD ** (-0.5)
    for start in range(0, q_ref.shape[1], LANES):
        cols = slice(start, start + LANES)
        queries, keys, value_rows = q_ref[:, cols], k_ref[:, cols], v_ref[:, cols]
        grad_mixed = gmix_ref[:, cols]
        grad_q = jnp.zeros((rows, LANES), f32)
        grad_k = jnp.zeros((rows, LANES), f32)
        grad_v = jnp.zeros((rows, LANES), f32)
        for mask in heads:
            one_q = jnp.where(mask, queries, 0).astype(bf16)
            one_g = jnp.where(mask, grad_mixed, 0).astype(bf16)
            probs = head_probs(one_q, keys, inside)
            grad_v = grad_v + dot(probs.astype(bf16), one_g, 0, 0)
            grad_attn = dot(one_g, value_rows, 1, 1)
            delta = jnp.sum(probs * grad_attn, axis=-1, keepdims=True)
            grad_scores = (probs * (grad_attn - delta)).astype(bf16)
            grad_q = jnp.where(mask, dot(grad_scores, keys, 1, 0), grad_q)
            grad_k = grad_k + dot(grad_scores, one_q, 0, 0)
        gq_ref[:, cols] = (grad_q * scale).astype(bf16)
        gk_ref[:, cols] = (grad_k * scale).astype(bf16)
        gv_ref[:, cols] = grad_v.astype(bf16)
    normed = norm_ref[...]
    total = None
    for part, ref in enumerate((gq_ref, gk_ref, gv_ref)):
        grads = ref[...]
        dw_ref[part] = dot(normed, grads, 0, 0).astype(bf16)
        term = dot(grads, w_ref[part], 1, 1)
        total = term if total is None else total + term
    part_ref[...] = total.astype(bf16)
    db_ref[0:1, :] = jnp.sum(gq_ref[...].astype(f32), axis=0, keepdims=True)
    db_ref[1:2, :] = jnp.sum(gv_ref[...].astype(f32), axis=0, keepdims=True)


def first_kernel(tok_ref, gain_ref, grad_ref, resid_ref, out_ref, small_ref):
    normal, rstd = norm_parts(tok_ref[...].astype(f32))
    grad = grad_ref[...].astype(f32)
    out_ref[...] = resid_ref[...] + norm_back(grad, normal, rstd, gain_ref[...])
    small_ref[0:1, :] = jnp.sum(grad * normal, axis=0, keepdims=True)
    small_ref[1:2, :] = jnp.sum(grad, axis=0, keepdims=True)


def on_device(
    tokens,
    gain_attn,
    shift_attn,
    w_qkv,
    b_qv,
    w_out,
    b_out,
    gain_moe,
    shift_moe,
    w_router,
    w_in,
    b_in,
    w_back,
    b_back,
    routes,
    d_out,
):
    groups = lax.axis_size("expert")
    blocks = lax.axis_size("tensor")
    rows, width = tokens.shape
    top = routes.shape[1]
    experts = w_router.shape[1]
    capacity = (top * rows * 16 // (10 * experts) + 7) // 8 * 8
    slots = experts * capacity
    local = w_qkv.shape[2]
    piece = width // blocks
    half = width // 2
    hidden = w_in.shape[2]
    row = lambda vec: vec.reshape(1, -1)
    tensor_id = lax.axis_index("tensor").astype(jnp.int32)
    expert_id = lax.axis_index("expert").astype(jnp.int32)
    ids = jnp.stack([tensor_id, expert_id])

    place, grad_send = call(
        functools.partial(route_kernel, experts=experts, capacity=capacity),
        [sds((rows, slots), bf16), sds((slots, piece), bf16)],
        [ids, routes, d_out],
        2 * rows * slots * piece,
        scalars=1,
    )
    grad_came = lax.all_to_all(
        grad_send.reshape(experts, capacity, piece), "expert", 0, 0, tiled=True
    ).reshape(slots, piece)
    w_out_all = lax.all_gather(w_out, "tensor", axis=0, tiled=False)

    normed, queries, keys, value_rows, mixed = call(
        attend_kernel,
        [sds((rows, width), bf16)] + [sds((rows, local), bf16)] * 4,
        [tokens, row(gain_attn), row(shift_attn), w_qkv, b_qv],
        6 * rows * width * local,
    )
    mixed_all = lax.all_gather(mixed, "tensor", axis=0, tiled=False)
    residual, second_low, router_probs, send = call(
        middle_kernel,
        [
            sds((rows, width), f32),
            sds((rows, width), bf16),
            sds((rows, experts), f32),
            sds((slots, half), bf16),
        ],
        [
            ids,
            mixed_all,
            w_out_all,
            tokens,
            row(b_out),
            row(gain_moe),
            row(shift_moe),
            w_router,
            place,
        ],
        2 * rows * width * width + 2 * rows * slots * half,
        scalars=1,
    )

    own = lax.all_to_all(
        send.reshape(experts, capacity, half), "expert", 0, 0, tiled=True
    ).reshape(slots, half)
    other = swap(own, "tensor", 1)
    grad_all = gather_tensor(grad_came)
    grad_rows = jnp.concatenate([grad_all[b] for b in range(blocks)], axis=1)
    unscaled = dot(grad_rows, w_back[0], 1, 1)

    tile = 256
    steps = slots // tile

    def by_row(cols):
        return pl.BlockSpec((tile, cols), lambda i: (i, 0))

    def whole(shape):
        return pl.BlockSpec(shape, lambda i: (0,) * len(shape))

    smem = pl.BlockSpec(memory_space=pltpu.SMEM)
    outs = call(
        functools.partial(expert_kernel, blocks=blocks),
        [sds((slots, piece), bf16)] * blocks
        + [
            sds((slots, hidden), bf16),
            sds((slots, hidden), bf16),
            sds((slots, width), bf16),
            sds((slots, 1), f32),
            sds((slots, 1), f32),
            sds((1, hidden), f32),
            sds((1, width), f32),
        ],
        [ids, own, other, grad_rows, unscaled, w_in[0], b_in, b_back, w_router],
        4 * slots * width * hidden,
        grid=(steps,),
        in_specs=[
            smem,
            by_row(half),
            by_row(half),
            by_row(width),
            by_row(hidden),
            whole((width, hidden)),
            whole((1, hidden)),
            whole((1, width)),
            whole((width, experts)),
        ],
        out_specs=[by_row(piece)] * blocks
        + [
            by_row(hidden),
            by_row(hidden),
            by_row(width),
            by_row(1),
            by_row(1),
            whole((1, hidden)),
            whole((1, width)),
        ],
    )
    grad_pieces = outs[:blocks]
    activated, grad_pre, grad_y, gate, gate_grads, d_b_in, d_b_back = outs[blocks:]

    gate_grads = butterfly(gate_grads.reshape(experts, capacity), "tensor")
    gate_grads = lax.all_to_all(gate_grads, "expert", 0, 0, tiled=True).reshape(1, slots)
    home = lax.all_to_all(
        scatter_tensor(grad_pieces).reshape(experts, capacity, piece), "expert", 0, 0, tiled=True
    ).reshape(slots, piece)
    dispatch = dot(place, home, 1, 0).astype(bf16)
    dispatch_all = lax.all_gather(dispatch, "tensor", axis=0, tiled=False)

    out_pieces = call(
        back_kernel,
        [sds((slots, piece), bf16)] * blocks,
        [ids, activated, gate, w_back[0], b_back],
        2 * slots * width * hidden,
        grid=(steps,),
        in_specs=[smem, by_row(hidden), by_row(1), whole((hidden, width)), whole((1, width))],
        out_specs=[by_row(piece)] * blocks,
    )
    out_home = lax.all_to_all(
        scatter_tensor(out_pieces).reshape(experts, capacity, piece), "expert", 0, 0, tiled=True
    ).reshape(slots, piece)
    mixture = dot(place, out_home, 1, 0).astype(bf16)
    mixture = lax.all_gather(mixture, "tensor", axis=1, tiled=True).astype(f32)
    activations = (residual + mixture).astype(bf16)

    d_w_back = dot(activated, grad_y, 0, 0)[None]
    side = tensor_id & 1
    rows_in = jnp.where(
        side == 0,
        jnp.concatenate([own, other], axis=1),
        jnp.concatenate([other, own], axis=1),
    )
    d_w_in = dot(rows_in, grad_pre, 0, 0)[None]

    grad_resid, d_w_out, grad_mixed, small = call(
        functools.partial(residual_kernel, capacity=capacity),
        [
            sds((rows, width), f32),
            sds((local, width), bf16),
            sds((rows, local), bf16),
            sds((experts + 3, width), f32),
        ],
        [
            dispatch_all,
            gate_grads,
            place,
            router_probs,
            second_low,
            w_router,
            residual,
            row(gain_moe),
            d_out,
            w_out,
            mixed,
        ],
        4 * rows * width * local,
    )
    d_w_qkv, d_b_qv, part, _, _, _ = call(
        attend_back_kernel,
        [
            sds((3, width, local), bf16),
            sds((2, local), f32),
            sds((rows, width), bf16),
            sds((rows, local), bf16),
            sds((rows, local), bf16),
            sds((rows, local), bf16),
        ],
        [queries, keys, value_rows, grad_mixed, normed, w_qkv],
        12 * rows * width * local,
    )
    order = bits_of(groups)
    d_w_out = sum_experts(d_w_out, order)
    d_w_qkv = [sum_experts(d_w_qkv[i], order) for i in range(3)]

    grad_normed = butterfly(part, "tensor")
    d_tokens, first_small = call(
        first_kernel,
        [sds((rows, width), f32), sds((2, width), f32)],
        [tokens, row(gain_attn), grad_normed, grad_resid],
        rows * width,
    )
    bias_row = jnp.pad(d_b_qv, ((0, 0), (0, width - local)))
    packed = jnp.concatenate([small, first_small, bias_row], axis=0).astype(bf16)
    packed = butterfly(packed, "expert").astype(f32)
    return (
        activations,
        d_tokens,
        packed[experts + 3],
        packed[experts + 4],
        jnp.stack(d_w_qkv).astype(f32),
        packed[experts + 5 : experts + 7, :local],
        d_w_out.astype(f32),
        packed[experts + 2],
        packed[experts],
        packed[experts + 1],
        packed[:experts].T,
        d_w_in,
        d_b_in,
        d_w_back,
        d_b_back,
    )


def solution(mesh):
    in_specs = (
        P("expert", None),
        P(),
        P(),
        P(None, None, "tensor"),
        P(None, "tensor"),
        P("tensor", None),
        P(),
        P(),
        P(),
        P(),
        P("expert", None, "tensor"),
        P("expert", "tensor"),
        P("expert", "tensor", None),
        P("expert", None),
        P("expert", None),
        P("expert", None),
    )
    out_specs = (
        P("expert", None),
        P("expert", None),
        P(),
        P(),
        P(None, None, "tensor"),
        P(None, "tensor"),
        P("tensor", None),
        P(),
        P(),
        P(),
        P(),
        P("expert", None, "tensor"),
        P("expert", "tensor"),
        P("expert", "tensor", None),
        P("expert", None),
    )
    return jax.shard_map(
        on_device, mesh=mesh, in_specs=in_specs, out_specs=out_specs, check_vma=False
    )
```

```python
import functools

import jax
import jax.numpy as jnp
from jax import lax
from jax.experimental import pallas as pl
from jax.experimental.pallas import tpu as pltpu
from jax.sharding import PartitionSpec as P

HD = 64
SEQ = 197
LANES = 128
VMEM_LIMIT = 52 * 1024 * 1024
EXTRA = 16

epsilon = 1e-06
f32 = jnp.float32
bf16 = jnp.bfloat16


def dot(left, right, left_dim, right_dim, precision=None):
    return lax.dot_general(
        left,
        right,
        (((left_dim,), (right_dim,)), ((), ())),
        precision=precision,
        preferred_element_type=f32,
    )


def call(body, outs, ins, flops, grid=None, in_specs=None, out_specs=None, scalars=0, scratch=()):
    specs = {"scratch_shapes": list(scratch)}
    if grid is not None:
        specs["grid"] = grid
        specs["in_specs"] = in_specs
        specs["out_specs"] = out_specs
    else:
        specs["in_specs"] = [
            pl.BlockSpec(memory_space=pltpu.SMEM if i < scalars else pltpu.VMEM)
            for i in range(len(ins))
        ]
        specs["out_specs"] = [pl.BlockSpec(memory_space=pltpu.VMEM) for _ in outs]
    moved = sum(a.size * a.dtype.itemsize for a in list(ins) + list(outs))
    return pl.pallas_call(
        body,
        out_shape=outs,
        compiler_params=pltpu.CompilerParams(vmem_limit_bytes=VMEM_LIMIT),
        cost_estimate=pl.CostEstimate(flops=flops, bytes_accessed=moved, transcendentals=0),
        **specs,
    )(*ins)


def sds(shape, dtype):
    return jax.ShapeDtypeStruct(shape, dtype)


def swap(values, axis, bit):
    count = lax.axis_size(axis)
    return lax.ppermute(values, axis, [(i, i ^ bit) for i in range(count)])


def bits_of(count):
    return [1 << i for i in range(count.bit_length() - 1)]


def gather_tensor(values, diagonal=False):
    count = lax.axis_size("tensor")
    held = {0: values}
    for bit in reversed(bits_of(count)):
        step = bit ^ 1 if diagonal and bit > 1 else bit
        for key in list(held):
            held[key ^ step] = swap(held[key], "tensor", step)
    return [held[key] for key in range(count)]


def add(left, right):
    return (left.astype(f32) + right.astype(f32)).astype(left.dtype)


def scatter_step(held, bit):
    kept = {}
    for key in sorted(held):
        if not key & bit:
            kept[key] = add(held[key], swap(held[key | bit], "tensor", bit))
    return kept


def butterfly(values, axis):
    for bit in bits_of(lax.axis_size(axis)):
        came = swap(values, axis, bit)
        values = add(values, came)
    return values


def sum_experts(values, order):
    index = lax.axis_index("expert")
    for bit in order:
        half = values.shape[0] // 2
        side = (index & bit) // bit
        keep = lax.dynamic_slice_in_dim(values, side * half, half, 0)
        send = lax.dynamic_slice_in_dim(values, (1 - side) * half, half, 0)
        came = swap(send, "expert", bit)
        values = (keep.astype(f32) + came.astype(f32)).astype(bf16)
    for bit in reversed(order):
        side = (index & bit) // bit
        came = swap(values, "expert", bit)
        values = jnp.where(
            side == 0,
            jnp.concatenate([values, came], 0),
            jnp.concatenate([came, values], 0),
        )
    return values


def norm_parts(values):
    center = values - jnp.mean(values, axis=-1, keepdims=True)
    variance = jnp.mean(center * center, axis=-1, keepdims=True)
    rstd = lax.rsqrt(variance + epsilon)
    return center * rstd, rstd


def norm_back(grad, normal, rstd, gain):
    scaled = grad * gain
    mean_g = jnp.mean(scaled, axis=-1, keepdims=True)
    mean_gn = jnp.mean(scaled * normal, axis=-1, keepdims=True)
    return rstd * (scaled - mean_g - normal * mean_gn)


def same_image(rows):
    left = lax.broadcasted_iota(jnp.int32, (rows, rows), 0)
    right = lax.broadcasted_iota(jnp.int32, (rows, rows), 1)
    left_id = jnp.zeros((rows, rows), jnp.int32)
    right_id = jnp.zeros((rows, rows), jnp.int32)
    for edge in range(SEQ, rows, SEQ):
        left_id = left_id + (left >= edge).astype(jnp.int32)
        right_id = right_id + (right >= edge).astype(jnp.int32)
    return left_id == right_id


def head_probs(queries, keys, inside):
    scores = dot(queries, keys, 1, 1) * (HD ** (-0.5))
    scores = jnp.where(inside, scores, -1e30)
    top = jnp.max(scores, axis=-1, keepdims=True)
    powers = jnp.exp(scores - top)
    return powers * (1.0 / jnp.sum(powers, axis=-1, keepdims=True))


def lane_heads(rows):
    lane = lax.broadcasted_iota(jnp.int32, (rows, LANES), 1)
    return [(lane // HD) == head for head in range(LANES // HD)]


def attend_kernel(tok_ref, gain_ref, shift_ref, w_ref, b_ref, norm_ref, q_ref, k_ref, v_ref, mix_ref):
    rows = tok_ref.shape[0]
    normal, _ = norm_parts(tok_ref[...].astype(f32))
    normed = (normal * gain_ref[...] + shift_ref[...]).astype(bf16)
    norm_ref[...] = normed
    q_ref[...] = (dot(normed, w_ref[0], 1, 0) + b_ref[0:1, :]).astype(bf16)
    k_ref[...] = dot(normed, w_ref[1], 1, 0).astype(bf16)
    v_ref[...] = (dot(normed, w_ref[2], 1, 0) + b_ref[1:2, :]).astype(bf16)
    inside = same_image(rows)
    heads = lane_heads(rows)
    for start in range(0, q_ref.shape[1], LANES):
        cols = slice(start, start + LANES)
        queries, keys, value_rows = q_ref[:, cols], k_ref[:, cols], v_ref[:, cols]
        mixed = jnp.zeros((rows, LANES), f32)
        for mask in heads:
            probs = head_probs(jnp.where(mask, queries, 0).astype(bf16), keys, inside)
            mixed = jnp.where(mask, dot(probs.astype(bf16), value_rows, 1, 0), mixed)
        mix_ref[:, cols] = mixed.astype(bf16)


def slot_numbers(named, earlier, ids, axis, stride):
    numbers = []
    for mask in named:
        slot = jnp.sum(jnp.where(mask, earlier, 0.0), axis=axis, keepdims=True).astype(jnp.int32)
        owner = jnp.sum(jnp.where(mask, ids, 0), axis=axis, keepdims=True)
        numbers.append(owner * stride + slot)
    return numbers


def one_hot(targets, shape, axis):
    ids = lax.broadcasted_iota(jnp.int32, shape, axis)
    table = jnp.zeros(shape, f32)
    for target in targets:
        table = jnp.where(ids == target, 1.0, table)
    return table.astype(bf16)


def route_kernel(
    idx_ref,
    routes_ref,
    flipped_ref,
    dout_ref,
    plain_ref,
    padded_ref,
    dispatch_ref,
    send_ref,
    *,
    experts,
    capacity,
):
    rows = plain_ref.shape[0]
    width = send_ref.shape[1]
    top = routes_ref.shape[1]
    first = lax.broadcasted_iota(jnp.int32, (rows, rows), 0)
    second = lax.broadcasted_iota(jnp.int32, (rows, rows), 1)

    ids = lax.broadcasted_iota(jnp.int32, (experts, rows), 0)
    named = [flipped_ref[k : k + 1, :] == ids for k in range(top)]
    tally = sum(m.astype(f32) for m in named).astype(bf16)
    earlier = dot(tally, (first < second).astype(f32).astype(bf16), 1, 0)
    numbers = slot_numbers(named, earlier, ids, 0, capacity)
    dispatch_ref[...] = one_hot(numbers, dispatch_ref.shape, 0)
    start = pl.multiple_of(idx_ref[0] * width, LANES)
    send_ref[...] = dot(dispatch_ref[...], dout_ref[:, pl.ds(start, width)], 1, 0).astype(bf16)

    ids = lax.broadcasted_iota(jnp.int32, (rows, experts), 1)
    named = [routes_ref[:, k : k + 1] == ids for k in range(top)]
    tally = sum(m.astype(f32) for m in named).astype(bf16)
    earlier = dot((second < first).astype(f32).astype(bf16), tally, 1, 0)
    for ref, stride in ((plain_ref, capacity), (padded_ref, capacity + EXTRA)):
        ref[...] = one_hot(slot_numbers(named, earlier, ids, 1, stride), ref.shape, 1)


def middle_kernel(*refs, blocks):
    idx_ref, refs = refs[0], refs[1:]
    mix_refs, w_refs, refs = refs[:blocks], refs[blocks : 2 * blocks], refs[2 * blocks :]
    tok_ref, bias_ref, gain_ref, shift_ref, router_ref, dispatch_ref = refs[:6]
    resid_ref, second_ref, probs_ref, send_ref, terms_ref = refs[6:]
    width = send_ref.shape[1]
    for key in range(blocks):
        terms_ref[key] = dot(mix_refs[key][...], w_refs[key][...], 1, 0)
    terms = [terms_ref[key] for key in range(blocks)]
    while len(terms) > 1:
        terms = [terms[i] + terms[i + 1] for i in range(0, len(terms), 2)]
    residual = tok_ref[...].astype(f32) + terms[0] + bias_ref[...]
    resid_ref[...] = residual
    normal, _ = norm_parts(residual)
    second_ref[...] = (normal * gain_ref[...] + shift_ref[...]).astype(bf16)
    start = pl.multiple_of((idx_ref[0] & 1) * width, LANES)
    send_ref[...] = dot(dispatch_ref[...], second_ref[:, pl.ds(start, width)], 1, 0).astype(bf16)
    logits = dot(second_ref[...], router_ref[...], 1, 0)
    powers = jnp.exp(logits - jnp.max(logits, axis=-1, keepdims=True))
    probs_ref[...] = powers / jnp.sum(powers, axis=-1, keepdims=True)


def early_kernel(*refs, blocks):
    idx_ref, piece_refs, w_ref = refs[0], refs[1 : 1 + blocks], refs[1 + blocks]
    rows_ref, unscaled_ref = refs[2 + blocks :]
    piece = piece_refs[0].shape[-1]
    for key, piece_ref in enumerate(piece_refs):
        cols = pl.ds(pl.multiple_of((idx_ref[0] ^ key) * piece, LANES), piece)
        rows_ref[:, cols] = piece_ref[...]
    unscaled_ref[...] = dot(rows_ref[...], w_ref[...], 1, 1)


def expert_kernel(
    idx_ref,
    own_ref,
    other_ref,
    grad_ref,
    unscaled_ref,
    w_in_ref,
    b_in_ref,
    b_back_ref,
    router_ref,
    *outs,
    blocks,
):
    piece_refs = outs[:blocks]
    act_ref, pre_ref, grady_ref, gate_ref, dbin_ref, dbback_ref = outs[blocks:]
    count, capacity = piece_refs[0].shape[0], piece_refs[0].shape[1] - EXTRA
    tensor_id, expert_id = idx_ref[0], idx_ref[1]
    side = tensor_id & 1
    width = w_in_ref.shape[0] // 2
    piece = w_in_ref.shape[0] // blocks
    own, other = own_ref[...], other_ref[...]
    low_half = jnp.where(side == 0, own, other)
    high_half = jnp.where(side == 0, other, own)
    logits = dot(low_half, router_ref[0:width, :], 1, 0) + dot(
        high_half, router_ref[width:, :], 1, 0
    )
    powers = jnp.exp(logits - jnp.max(logits, axis=-1, keepdims=True))
    ids = lax.broadcasted_iota(jnp.int32, logits.shape, 1)
    gate = jnp.sum(jnp.where(ids == expert_id, powers, 0.0), axis=-1, keepdims=True) / jnp.sum(
        powers, axis=-1, keepdims=True
    )
    gate_ref[...] = gate
    pre_act = (
        dot(low_half, w_in_ref[0:width, :], 1, 0)
        + dot(high_half, w_in_ref[width:, :], 1, 0)
        + b_in_ref[...]
    )
    cdf = 0.5 * (1.0 + lax.erf(pre_act * (2.0**-0.5)))
    density = jnp.exp(-0.5 * pre_act * pre_act) * 0.3989422804014327
    act = (pre_act * cdf).astype(bf16)
    act_ref[...] = act
    unscaled = unscaled_ref[...]
    grad_pre = (gate * unscaled * (cdf + pre_act * density)).astype(bf16)
    pre_ref[...] = grad_pre
    grad_rows = grad_ref[...].astype(f32)
    gate_grads = jnp.sum(act.astype(f32) * unscaled, axis=1, keepdims=True) + jnp.sum(
        grad_rows * b_back_ref[...], axis=1, keepdims=True
    ) * (1.0 / blocks)
    gate_grads = jnp.broadcast_to(gate_grads, (gate_grads.shape[0], LANES)).T
    grad_y = (gate * grad_rows).astype(bf16)
    grady_ref[...] = grad_y

    @pl.when(pl.program_id(0) == 0)
    def _():
        dbin_ref[...] = jnp.zeros_like(dbin_ref)
        dbback_ref[...] = jnp.zeros_like(dbback_ref)

    dbin_ref[...] += jnp.sum(grad_pre.astype(f32), axis=0, keepdims=True)
    dbback_ref[...] += jnp.sum(grad_y.astype(f32), axis=0, keepdims=True)
    for key, piece_ref in enumerate(piece_refs):
        start = pl.multiple_of((tensor_id ^ key) * piece, LANES)
        rows = dot(grad_pre, w_in_ref[pl.ds(start, piece), :], 1, 1)
        for source in range(count):
            part = slice(source * capacity, (source + 1) * capacity)
            piece_ref[source, 0:capacity, :] = rows[part, :].astype(bf16)
            piece_ref[source, capacity : capacity + EXTRA, :] = jnp.zeros((EXTRA, piece), bf16)
            for first in range(0, capacity, piece):
                lanes = min(piece, capacity - first)
                place = capacity + first // piece
                here = source * capacity + first
                piece_ref[source, place : place + 1, 0:lanes] = gate_grads[
                    0:1, here : here + lanes
                ].astype(bf16)


def back_kernel(idx_ref, act_ref, gate_ref, w_ref, bias_ref, *piece_refs):
    blocks = len(piece_refs)
    piece = piece_refs[0].shape[-1]
    for key, piece_ref in enumerate(piece_refs):
        cols = pl.ds(pl.multiple_of((idx_ref[0] ^ key) * piece, LANES), piece)
        rows = dot(act_ref[...], w_ref[:, cols], 1, 0) + bias_ref[:, cols] * (1.0 / blocks)
        piece_ref[...] = (gate_ref[...] * rows).astype(bf16)


def combine_kernel(place_ref, home_ref, out_ref):
    out_ref[...] = dot(place_ref[...], home_ref[...], 1, 0).astype(bf16)


def finish_kernel(idx_ref, resid_ref, *refs):
    piece_refs, out_ref = refs[:-1], refs[-1]
    piece = piece_refs[0].shape[1]
    for key, piece_ref in enumerate(piece_refs):
        cols = pl.ds(pl.multiple_of((idx_ref[0] ^ key) * piece, LANES), piece)
        out_ref[:, cols] = (resid_ref[:, cols] + piece_ref[...].astype(f32)).astype(bf16)


def residual_kernel(*refs, blocks, capacity):
    idx_ref, piece_refs, refs = refs[0], refs[1 : 1 + blocks], refs[1 + blocks :]
    residual_body(idx_ref, piece_refs, *refs, capacity=capacity)


def residual_body(
    idx_ref,
    piece_refs,
    gg_ref,
    place_ref,
    probs_ref,
    second_ref,
    router_ref,
    resid_ref,
    gain_ref,
    dout_ref,
    w_ref,
    mix_ref,
    grad_ref,
    dw_ref,
    gmix_ref,
    small_ref,
    disp_ref,
    *,
    capacity,
):
    probs = probs_ref[...]
    experts = probs.shape[1]
    slots = place_ref.shape[1]
    piece = piece_refs[0].shape[1]
    stride = capacity + EXTRA
    lane = lax.broadcasted_iota(jnp.int32, (experts, slots), 1)
    first = lax.broadcasted_iota(jnp.int32, (experts, slots), 0) * stride
    segment = (lane >= first) & (lane < first + capacity)
    gate_rows = jnp.where(segment, jnp.broadcast_to(gg_ref[...], (experts, slots)), 0.0)
    grad_probs = dot(place_ref[...], gate_rows.astype(bf16), 1, 1)
    for key, piece_ref in enumerate(piece_refs):
        cols = pl.ds(pl.multiple_of((idx_ref[0] ^ key) * piece, LANES), piece)
        disp_ref[:, cols] = piece_ref[...]
    grad_logits = (
        probs * (grad_probs - jnp.sum(probs * grad_probs, axis=1, keepdims=True))
    ).astype(bf16)
    second_grad = disp_ref[...].astype(f32) + dot(grad_logits, router_ref[...], 1, 1)
    normal, rstd = norm_parts(resid_ref[...])
    grad_resid = dout_ref[...].astype(f32) + norm_back(second_grad, normal, rstd, gain_ref[...])
    grad_ref[...] = grad_resid
    branch = grad_resid.astype(bf16)
    gmix_ref[...] = dot(branch, w_ref[...], 1, 1).astype(bf16)
    dw_ref[...] = dot(mix_ref[...], branch, 0, 0).astype(bf16)
    small_ref[0:experts, :] = dot(grad_logits, second_ref[...], 0, 0)
    small_ref[experts : experts + 1, :] = jnp.sum(second_grad * normal, axis=0, keepdims=True)
    small_ref[experts + 1 : experts + 2, :] = jnp.sum(second_grad, axis=0, keepdims=True)
    small_ref[experts + 2 : experts + 3, :] = jnp.sum(grad_resid, axis=0, keepdims=True)


def attend_back_kernel(
    q_ref, k_ref, v_ref, gmix_ref, norm_ref, w_ref, dw_ref, db_ref, part_ref, gq_ref, gk_ref, gv_ref
):
    rows = q_ref.shape[0]
    inside = same_image(rows)
    heads = lane_heads(rows)
    scale = HD ** (-0.5)
    for start in range(0, q_ref.shape[1], LANES):
        cols = slice(start, start + LANES)
        queries, keys, value_rows = q_ref[:, cols], k_ref[:, cols], v_ref[:, cols]
        grad_mixed = gmix_ref[:, cols]
        grad_q = jnp.zeros((rows, LANES), f32)
        grad_k = jnp.zeros((rows, LANES), f32)
        grad_v = jnp.zeros((rows, LANES), f32)
        for mask in heads:
            one_q = jnp.where(mask, queries, 0).astype(bf16)
            one_g = jnp.where(mask, grad_mixed, 0).astype(bf16)
            probs = head_probs(one_q, keys, inside)
            grad_v = grad_v + dot(probs.astype(bf16), one_g, 0, 0)
            grad_attn = dot(one_g, value_rows, 1, 1)
            delta = jnp.sum(probs * grad_attn, axis=-1, keepdims=True)
            grad_scores = (probs * (grad_attn - delta)).astype(bf16)
            grad_q = jnp.where(mask, dot(grad_scores, keys, 1, 0), grad_q)
            grad_k = grad_k + dot(grad_scores, one_q, 0, 0)
        gq_ref[:, cols] = (grad_q * scale).astype(bf16)
        gk_ref[:, cols] = (grad_k * scale).astype(bf16)
        gv_ref[:, cols] = grad_v.astype(bf16)
    normed = norm_ref[...]
    total = None
    for part, ref in enumerate((gq_ref, gk_ref, gv_ref)):
        grads = ref[...]
        dw_ref[part] = dot(normed, grads, 0, 0).astype(bf16)
        term = dot(grads, w_ref[part], 1, 1)
        total = term if total is None else total + term
    part_ref[...] = total.astype(bf16)
    db_ref[0:1, :] = jnp.sum(gq_ref[...].astype(f32), axis=0, keepdims=True)
    db_ref[1:2, :] = jnp.sum(gv_ref[...].astype(f32), axis=0, keepdims=True)


def first_kernel(tok_ref, gain_ref, grad_ref, resid_ref, out_ref, small_ref):
    normal, rstd = norm_parts(tok_ref[...].astype(f32))
    grad = grad_ref[...].astype(f32)
    out_ref[...] = resid_ref[...] + norm_back(grad, normal, rstd, gain_ref[...])
    small_ref[0:1, :] = jnp.sum(grad * normal, axis=0, keepdims=True)
    small_ref[1:2, :] = jnp.sum(grad, axis=0, keepdims=True)


def on_device(
    tokens,
    gain_attn,
    shift_attn,
    w_qkv,
    b_qv,
    w_out,
    b_out,
    gain_moe,
    shift_moe,
    w_router,
    w_in,
    b_in,
    w_back,
    b_back,
    routes,
    d_out,
):
    groups = lax.axis_size("expert")
    blocks = lax.axis_size("tensor")
    rows, width = tokens.shape
    top = routes.shape[1]
    experts = w_router.shape[1]
    capacity = (top * rows * 16 // (10 * experts) + 7) // 8 * 8
    slots = experts * capacity
    local = w_qkv.shape[2]
    piece = width // blocks
    half = width // 2
    hidden = w_in.shape[2]
    row = lambda vec: vec.reshape(1, -1)
    tensor_id = lax.axis_index("tensor").astype(jnp.int32)
    expert_id = lax.axis_index("expert").astype(jnp.int32)
    ids = jnp.stack([tensor_id, expert_id])
    stride = capacity + EXTRA
    row_bits = bits_of(blocks)

    plain, padded, dispatch_place, grad_send = call(
        functools.partial(route_kernel, experts=experts, capacity=capacity),
        [
            sds((rows, slots), bf16),
            sds((rows, experts * stride), bf16),
            sds((slots, rows), bf16),
            sds((slots, piece), bf16),
        ],
        [ids, routes, routes.T, d_out],
        2 * rows * slots * piece,
        scalars=1,
    )
    w_out_all = gather_tensor(w_out, diagonal=True)
    tokens_in, grad_send = lax.optimization_barrier((tokens, grad_send))
    grad_came = lax.all_to_all(
        grad_send.reshape(experts, capacity, piece), "expert", 0, 0, tiled=True
    ).reshape(slots, piece)

    normed, queries, keys, value_rows, mixed = call(
        attend_kernel,
        [sds((rows, width), bf16)] + [sds((rows, local), bf16)] * 4,
        [tokens_in, row(gain_attn), row(shift_attn), w_qkv, b_qv],
        6 * rows * width * local,
    )
    mixed_all = gather_tensor(mixed)
    residual, second_low, router_probs, send = call(
        functools.partial(middle_kernel, blocks=blocks),
        [
            sds((rows, width), f32),
            sds((rows, width), bf16),
            sds((rows, experts), f32),
            sds((slots, half), bf16),
        ],
        [
            ids,
            *mixed_all,
            *w_out_all,
            tokens,
            row(b_out),
            row(gain_moe),
            row(shift_moe),
            w_router,
            dispatch_place,
        ],
        2 * rows * width * width + 2 * rows * slots * half,
        scalars=1,
        scratch=[pltpu.VMEM((blocks, rows, width), f32)],
    )

    own = lax.all_to_all(
        send.reshape(experts, capacity, half), "expert", 0, 0, tiled=True
    ).reshape(slots, half)
    smem = pl.BlockSpec(memory_space=pltpu.SMEM)
    count = max(1, min(experts, 320 // capacity))
    tile = count * capacity
    steps = slots // tile

    def whole(shape):
        return pl.BlockSpec(shape, lambda i: (0,) * len(shape))

    def by_row(cols):
        return pl.BlockSpec((tile, cols), lambda i: (i, 0))

    grad_rows, unscaled = call(
        functools.partial(early_kernel, blocks=blocks),
        [sds((slots, width), bf16), sds((slots, hidden), f32)],
        [ids, *gather_tensor(grad_came, diagonal=True), w_back[0]],
        2 * slots * width * hidden,
        grid=(steps,),
        in_specs=[smem] + [by_row(piece)] * blocks + [whole((hidden, width))],
        out_specs=[by_row(width), by_row(hidden)],
    )
    own, grad_rows, unscaled = lax.optimization_barrier((own, grad_rows, unscaled))
    other = swap(own, "tensor", 1)

    outs = call(
        functools.partial(expert_kernel, blocks=blocks),
        [sds((experts, stride, piece), bf16)] * blocks
        + [
            sds((slots, hidden), bf16),
            sds((slots, hidden), bf16),
            sds((slots, width), bf16),
            sds((slots, 1), f32),
            sds((1, hidden), f32),
            sds((1, width), f32),
        ],
        [ids, own, other, grad_rows, unscaled, w_in[0], b_in, b_back, w_router],
        4 * slots * width * hidden,
        grid=(steps,),
        in_specs=[
            smem,
            by_row(half),
            by_row(half),
            by_row(width),
            by_row(hidden),
            whole((width, hidden)),
            whole((1, hidden)),
            whole((1, width)),
            whole((width, experts)),
        ],
        out_specs=[pl.BlockSpec((count, stride, piece), lambda i: (i, 0, 0))] * blocks
        + [
            by_row(hidden),
            by_row(hidden),
            by_row(width),
            by_row(1),
            whole((1, hidden)),
            whole((1, width)),
        ],
    )
    held = scatter_step(dict(enumerate(outs[:blocks])), row_bits[0])
    activated, grad_pre, grad_y, gate, d_b_in, d_b_back = outs[blocks:]
    held, activated, grad_pre, grad_y = lax.optimization_barrier(
        (held, activated, grad_pre, grad_y)
    )

    out_pieces = call(
        back_kernel,
        [sds((slots, piece), bf16)] * blocks,
        [ids, activated, gate, w_back[0], b_back],
        2 * slots * width * hidden,
        grid=(steps,),
        in_specs=[smem, by_row(hidden), by_row(1), whole((hidden, width)), whole((1, width))],
        out_specs=[by_row(piece)] * blocks,
    )
    out_held = scatter_step(dict(enumerate(out_pieces)), row_bits[0])

    for bit in row_bits[1:]:
        held = scatter_step(held, bit)
    home = lax.all_to_all(held[0], "expert", 0, 0, tiled=True)
    for bit in row_bits[1:]:
        out_held = scatter_step(out_held, bit)

    d_w_back = dot(activated, grad_y, 0, 0)[None]
    side = tensor_id & 1
    rows_in = jnp.where(
        side == 0,
        jnp.concatenate([own, other], axis=1),
        jnp.concatenate([other, own], axis=1),
    )
    d_w_in = dot(rows_in, grad_pre, 0, 0)[None]
    home, d_w_back, d_w_in = lax.optimization_barrier((home, d_w_back, d_w_in))
    out_sent = out_held[0]
    dispatch = call(
        combine_kernel,
        [sds((rows, piece), bf16)],
        [padded, home.reshape(experts * stride, piece)],
        2 * rows * slots * piece,
    )[0]
    dispatch_all = gather_tensor(dispatch)
    gate_lines = -(-capacity // piece)
    gate_grads = home[:, capacity : capacity + gate_lines, :].reshape(experts, gate_lines * piece)
    gate_grads = jnp.pad(gate_grads[:, :capacity].astype(f32), ((0, 0), (0, EXTRA)))
    gate_grads = gate_grads.reshape(1, experts * stride)

    out_home = lax.all_to_all(
        out_sent.reshape(experts, capacity, piece), "expert", 0, 0, tiled=True
    ).reshape(slots, piece)
    mixture = call(
        combine_kernel, [sds((rows, piece), bf16)], [plain, out_home], 2 * rows * slots * piece
    )[0]
    activations = call(
        finish_kernel,
        [sds((rows, width), bf16)],
        [ids, residual, *gather_tensor(mixture)],
        rows * width,
        scalars=1,
    )[0]

    grad_resid, d_w_out, grad_mixed, small = call(
        functools.partial(residual_kernel, blocks=blocks, capacity=capacity),
        [
            sds((rows, width), f32),
            sds((local, width), bf16),
            sds((rows, local), bf16),
            sds((experts + 3, width), f32),
        ],
        [
            ids,
            *dispatch_all,
            gate_grads,
            padded,
            router_probs,
            second_low,
            w_router,
            residual,
            row(gain_moe),
            d_out,
            w_out,
            mixed,
        ],
        4 * rows * width * local,
        scalars=1,
        scratch=[pltpu.VMEM((rows, width), bf16)],
    )
    d_w_qkv, d_b_qv, partial_grad, _, _, _ = call(
        attend_back_kernel,
        [
            sds((3, width, local), bf16),
            sds((2, local), f32),
            sds((rows, width), bf16),
            sds((rows, local), bf16),
            sds((rows, local), bf16),
            sds((rows, local), bf16),
        ],
        [queries, keys, value_rows, grad_mixed, normed, w_qkv],
        12 * rows * width * local,
    )
    order = bits_of(groups)
    d_w_out = sum_experts(d_w_out, order)
    cut = 3 * width // 2
    d_w_qkv = d_w_qkv.reshape(3 * width, local)
    d_w_qkv = jnp.concatenate(
        [
            sum_experts(d_w_qkv[:cut], order),
            sum_experts(d_w_qkv[cut:], order[1:2] + order[:1] + order[2:]),
        ],
        axis=0,
    ).reshape(3, width, local)

    grad_normed = butterfly(partial_grad, "tensor")
    d_tokens, first_small = call(
        first_kernel,
        [sds((rows, width), f32), sds((2, width), f32)],
        [tokens, row(gain_attn), grad_normed, grad_resid],
        rows * width,
    )
    bias_row = jnp.pad(d_b_qv, ((0, 0), (0, width - local)))
    packed = jnp.concatenate([small, first_small, bias_row], axis=0).astype(bf16)
    packed = butterfly(packed, "expert").astype(f32)
    return (
        activations,
        d_tokens,
        packed[experts + 3],
        packed[experts + 4],
        d_w_qkv.astype(f32),
        packed[experts + 5 : experts + 7, :local],
        d_w_out.astype(f32),
        packed[experts + 2],
        packed[experts],
        packed[experts + 1],
        packed[:experts].T,
        d_w_in,
        d_b_in,
        d_w_back,
        d_b_back,
    )


def solution(mesh):
    in_specs = (
        P("expert", None),
        P(),
        P(),
        P(None, None, "tensor"),
        P(None, "tensor"),
        P("tensor", None),
        P(),
        P(),
        P(),
        P(),
        P("expert", None, "tensor"),
        P("expert", "tensor"),
        P("expert", "tensor", None),
        P("expert", None),
        P("expert", None),
        P("expert", None),
    )
    out_specs = (
        P("expert", None),
        P("expert", None),
        P(),
        P(),
        P(None, None, "tensor"),
        P(None, "tensor"),
        P("tensor", None),
        P(),
        P(),
        P(),
        P(),
        P("expert", None, "tensor"),
        P("expert", "tensor"),
        P("expert", "tensor", None),
        P("expert", None),
    )
    return jax.shard_map(
        on_device, mesh=mesh, in_specs=in_specs, out_specs=out_specs, check_vma=False
    )
```

```python
import functools

import jax
import jax.numpy as jnp
from jax import lax
from jax.experimental import pallas as pl
from jax.experimental.pallas import tpu as pltpu
from jax.sharding import PartitionSpec as P

HD = 64
SEQ = 197
LANES = 128
VMEM_LIMIT = 52 * 1024 * 1024
EXTRA = 16
MASKS = ((1, 2, 4), (2, 1, 5), (1, 3, 6))
FLOPS_PER_US = 1.15e9

epsilon = 1e-06
f32 = jnp.float32
bf16 = jnp.bfloat16


def dot(left, right, left_dim, right_dim, precision=None):
    return lax.dot_general(
        left,
        right,
        (((left_dim,), (right_dim,)), ((), ())),
        precision=precision,
        preferred_element_type=f32,
    )


def call(
    body, outs, ins, us, grid=None, in_specs=None, out_specs=None, scalars=0, scratch=(), after=()
):
    specs = {"scratch_shapes": list(scratch)}
    if grid is not None:
        specs["grid"] = grid
        specs["out_specs"] = out_specs
    else:
        in_specs = [
            pl.BlockSpec(memory_space=pltpu.SMEM if i < scalars else pltpu.VMEM)
            for i in range(len(ins))
        ]
        specs["out_specs"] = [pl.BlockSpec(memory_space=pltpu.VMEM) for _ in outs]
    specs["in_specs"] = in_specs + [pl.BlockSpec(memory_space=pl.ANY)] * len(after)
    used = len(ins)

    def run(*refs):
        body(*refs[:used], *refs[used + len(after) :])

    return pl.pallas_call(
        run,
        out_shape=outs,
        compiler_params=pltpu.CompilerParams(vmem_limit_bytes=VMEM_LIMIT),
        cost_estimate=pl.CostEstimate(
            flops=int(us * FLOPS_PER_US), bytes_accessed=0, transcendentals=0
        ),
        **specs,
    )(*ins, *after)


def sds(shape, dtype):
    return jax.ShapeDtypeStruct(shape, dtype)


def swap(values, axis, bit):
    count = lax.axis_size(axis)
    return lax.ppermute(values, axis, [(i, i ^ bit) for i in range(count)])


def bits_of(count):
    return [1 << i for i in range(count.bit_length() - 1)]


def gather_tensor(values, diagonal=False):
    count = lax.axis_size("tensor")
    held = {0: values}
    for bit in reversed(bits_of(count)):
        step = bit ^ 1 if diagonal and bit > 1 else bit
        for key in list(held):
            held[key ^ step] = swap(held[key], "tensor", step)
    return [held[key] for key in range(count)]


def add(left, right):
    return (left.astype(f32) + right.astype(f32)).astype(left.dtype)


def scatter_step(held, bit):
    kept = {}
    for key in sorted(held):
        if not key & bit:
            kept[key] = add(held[key], swap(held[key | bit], "tensor", bit))
    return kept


def scatter_sent(held, bits):
    for bit in bits[1:-1]:
        held = scatter_step(held, bit)
    if len(bits) == 1:
        return held
    return {0: held[0], 1: swap(held[bits[-1]], "tensor", bits[-1])}


def scatter_last(held, bits):
    return held[0] if len(bits) == 1 else add(held[0], held[1])


def butterfly(values, axis):
    for bit in bits_of(lax.axis_size(axis)):
        came = swap(values, axis, bit)
        values = add(values, came)
    return values


def chain_of(count, masks):
    masks = [m for m in masks if m < count]
    masks += bits_of(count)[len(masks) :]
    parity = lambda value: bin(value).count("1") % 2
    sides = []
    for step in range(len(masks)):
        wanted = [int(step == other) for other in range(len(masks))]
        fits = [d for d in range(count) if [parity(d & m) for m in masks] == wanted]
        sides.append(fits[0])
    return list(zip(masks, sides))


def side_of(bits):
    index = lax.axis_index("expert")
    total = sum(((index >> b) & 1 for b in range(bits.bit_length()) if (bits >> b) & 1))
    return (total & 1).astype(jnp.int32)


def reduce_experts(values, chain):
    sums = [values]
    for mask, bits in chain[1:]:
        half = values.shape[0] // 2
        side = side_of(bits)
        keep = lax.dynamic_slice_in_dim(values, side * half, half, 0)
        send = lax.dynamic_slice_in_dim(values, (1 - side) * half, half, 0)
        values = add(keep, swap(send, "expert", mask))
        sums.append(values)
    return sums


def spread_experts(values, chain, rider=None):
    count = 0 if rider is None else rider.shape[0]
    for mask, bits in reversed(chain):
        rows = values.shape[0]
        sent = values if rider is None else jnp.concatenate([values, rider], 0)
        came = swap(sent, "expert", mask)
        if rider is not None:
            rider = add(rider, came[rows : rows + count])
        came = came[:rows]
        if (mask, bits) == chain[0]:
            return values, came, rider
        values = jnp.where(
            side_of(bits) == 0,
            jnp.concatenate([values, came], 0),
            jnp.concatenate([came, values], 0),
        )


def norm_parts(values):
    center = values - jnp.mean(values, axis=-1, keepdims=True)
    variance = jnp.mean(center * center, axis=-1, keepdims=True)
    rstd = lax.rsqrt(variance + epsilon)
    return center * rstd, rstd


def norm_back(grad, normal, rstd, gain):
    scaled = grad * gain
    mean_g = jnp.mean(scaled, axis=-1, keepdims=True)
    mean_gn = jnp.mean(scaled * normal, axis=-1, keepdims=True)
    return rstd * (scaled - mean_g - normal * mean_gn)


def same_image(rows):
    left = lax.broadcasted_iota(jnp.int32, (rows, rows), 0)
    right = lax.broadcasted_iota(jnp.int32, (rows, rows), 1)
    left_id = jnp.zeros((rows, rows), jnp.int32)
    right_id = jnp.zeros((rows, rows), jnp.int32)
    for edge in range(SEQ, rows, SEQ):
        left_id = left_id + (left >= edge).astype(jnp.int32)
        right_id = right_id + (right >= edge).astype(jnp.int32)
    return left_id == right_id


def head_probs(queries, keys, inside):
    scores = dot(queries, keys, 1, 1) * (HD ** (-0.5))
    scores = jnp.where(inside, scores, -1e30)
    top = jnp.max(scores, axis=-1, keepdims=True)
    powers = jnp.exp(scores - top)
    return powers * (1.0 / jnp.sum(powers, axis=-1, keepdims=True))


def lane_heads(rows):
    lane = lax.broadcasted_iota(jnp.int32, (rows, LANES), 1)
    return [(lane // HD) == head for head in range(LANES // HD)]


def attend_kernel(tok_ref, gain_ref, shift_ref, w_ref, b_ref, norm_ref, q_ref, k_ref, v_ref, mix_ref):
    rows = tok_ref.shape[0]
    normal, _ = norm_parts(tok_ref[...].astype(f32))
    normed = (normal * gain_ref[...] + shift_ref[...]).astype(bf16)
    norm_ref[...] = normed
    q_ref[...] = (dot(normed, w_ref[0], 1, 0) + b_ref[0:1, :]).astype(bf16)
    k_ref[...] = dot(normed, w_ref[1], 1, 0).astype(bf16)
    v_ref[...] = (dot(normed, w_ref[2], 1, 0) + b_ref[1:2, :]).astype(bf16)
    inside = same_image(rows)
    heads = lane_heads(rows)
    for start in range(0, q_ref.shape[1], LANES):
        cols = slice(start, start + LANES)
        queries, keys, value_rows = q_ref[:, cols], k_ref[:, cols], v_ref[:, cols]
        mixed = jnp.zeros((rows, LANES), f32)
        for mask in heads:
            probs = head_probs(jnp.where(mask, queries, 0).astype(bf16), keys, inside)
            mixed = jnp.where(mask, dot(probs.astype(bf16), value_rows, 1, 0), mixed)
        mix_ref[:, cols] = mixed.astype(bf16)


def slot_numbers(named, earlier, ids, axis, stride):
    numbers = []
    for mask in named:
        slot = jnp.sum(jnp.where(mask, earlier, 0.0), axis=axis, keepdims=True).astype(jnp.int32)
        owner = jnp.sum(jnp.where(mask, ids, 0), axis=axis, keepdims=True)
        numbers.append(owner * stride + slot)
    return numbers


def one_hot(targets, shape, axis):
    ids = lax.broadcasted_iota(jnp.int32, shape, axis)
    table = jnp.zeros(shape, f32)
    for target in targets:
        table = jnp.where(ids == target, 1.0, table)
    return table.astype(bf16)


def route_kernel(idx_ref, flipped_ref, dout_ref, dispatch_ref, send_ref, *, experts, capacity):
    rows = dispatch_ref.shape[1]
    width = send_ref.shape[1]
    first = lax.broadcasted_iota(jnp.int32, (rows, rows), 0)
    second = lax.broadcasted_iota(jnp.int32, (rows, rows), 1)
    ids = lax.broadcasted_iota(jnp.int32, (experts, rows), 0)
    named = [flipped_ref[k : k + 1, :] == ids for k in range(flipped_ref.shape[0])]
    tally = sum(m.astype(f32) for m in named).astype(bf16)
    earlier = dot(tally, (first < second).astype(f32).astype(bf16), 1, 0)
    numbers = slot_numbers(named, earlier, ids, 0, capacity)
    dispatch_ref[...] = one_hot(numbers, dispatch_ref.shape, 0)
    start = pl.multiple_of(idx_ref[0] * width, LANES)
    send_ref[...] = dot(dispatch_ref[...], dout_ref[:, pl.ds(start, width)], 1, 0).astype(bf16)


def place_kernel(routes_ref, plain_ref, padded_ref, *, experts, capacity):
    rows = plain_ref.shape[0]
    first = lax.broadcasted_iota(jnp.int32, (rows, rows), 0)
    second = lax.broadcasted_iota(jnp.int32, (rows, rows), 1)
    ids = lax.broadcasted_iota(jnp.int32, (rows, experts), 1)
    named = [routes_ref[:, k : k + 1] == ids for k in range(routes_ref.shape[1])]
    tally = sum(m.astype(f32) for m in named).astype(bf16)
    earlier = dot((second < first).astype(f32).astype(bf16), tally, 1, 0)
    for ref, stride in ((plain_ref, capacity), (padded_ref, capacity + EXTRA)):
        ref[...] = one_hot(slot_numbers(named, earlier, ids, 1, stride), ref.shape, 1)


def middle_kernel(*refs, blocks):
    idx_ref, refs = refs[0], refs[1:]
    mix_refs, w_refs, refs = refs[:blocks], refs[blocks : 2 * blocks], refs[2 * blocks :]
    tok_ref, bias_ref, gain_ref, shift_ref, router_ref, dispatch_ref = refs[:6]
    resid_ref, second_ref, probs_ref, send_ref, terms_ref = refs[6:]
    width = send_ref.shape[1]
    for key in range(blocks):
        terms_ref[key] = dot(mix_refs[key][...], w_refs[key][...], 1, 0)
    terms = [terms_ref[key] for key in range(blocks)]
    while len(terms) > 1:
        terms = [terms[i] + terms[i + 1] for i in range(0, len(terms), 2)]
    residual = tok_ref[...].astype(f32) + terms[0] + bias_ref[...]
    resid_ref[...] = residual
    normal, _ = norm_parts(residual)
    second_ref[...] = (normal * gain_ref[...] + shift_ref[...]).astype(bf16)
    start = pl.multiple_of((idx_ref[0] & 1) * width, LANES)
    send_ref[...] = dot(dispatch_ref[...], second_ref[:, pl.ds(start, width)], 1, 0).astype(bf16)
    logits = dot(second_ref[...], router_ref[...], 1, 0)
    powers = jnp.exp(logits - jnp.max(logits, axis=-1, keepdims=True))
    probs_ref[...] = powers / jnp.sum(powers, axis=-1, keepdims=True)


def early_kernel(*refs, blocks):
    idx_ref, piece_refs = refs[0], refs[1 : 1 + blocks]
    w_ref, bias_ref, rows_ref, unscaled_ref, bias_dot_ref = refs[1 + blocks :]
    piece = piece_refs[0].shape[-1]
    for key, piece_ref in enumerate(piece_refs):
        cols = pl.ds(pl.multiple_of((idx_ref[0] ^ key) * piece, LANES), piece)
        rows_ref[:, cols] = piece_ref[...]
    unscaled_ref[...] = dot(rows_ref[...], w_ref[...], 1, 1)
    bias_dot_ref[...] = jnp.sum(
        rows_ref[...].astype(f32) * bias_ref[...], axis=1, keepdims=True
    ) * (1.0 / blocks)


def expert_kernel(
    idx_ref,
    own_ref,
    other_ref,
    grad_ref,
    unscaled_ref,
    bias_dot_ref,
    w_in_ref,
    b_in_ref,
    router_ref,
    *outs,
    blocks,
):
    piece_refs = outs[:blocks]
    act_ref, pre_ref, grady_ref, gate_ref, dbin_ref, dbback_ref = outs[blocks:]
    count, capacity = piece_refs[0].shape[0], piece_refs[0].shape[1] - EXTRA
    tensor_id, expert_id = idx_ref[0], idx_ref[1]
    side = tensor_id & 1
    width = w_in_ref.shape[0] // 2
    piece = w_in_ref.shape[0] // blocks
    own, other = own_ref[...], other_ref[...]
    low_half = jnp.where(side == 0, own, other)
    high_half = jnp.where(side == 0, other, own)
    logits = dot(low_half, router_ref[0:width, :], 1, 0) + dot(
        high_half, router_ref[width:, :], 1, 0
    )
    powers = jnp.exp(logits - jnp.max(logits, axis=-1, keepdims=True))
    ids = lax.broadcasted_iota(jnp.int32, logits.shape, 1)
    gate = jnp.sum(jnp.where(ids == expert_id, powers, 0.0), axis=-1, keepdims=True) / jnp.sum(
        powers, axis=-1, keepdims=True
    )
    gate_ref[...] = gate
    pre_act = (
        dot(low_half, w_in_ref[0:width, :], 1, 0)
        + dot(high_half, w_in_ref[width:, :], 1, 0)
        + b_in_ref[...]
    )
    cdf = 0.5 * (1.0 + lax.erf(pre_act * (2.0**-0.5)))
    density = jnp.exp(-0.5 * pre_act * pre_act) * 0.3989422804014327
    act = (pre_act * cdf).astype(bf16)
    act_ref[...] = act
    unscaled = unscaled_ref[...]
    grad_pre = (gate * unscaled * (cdf + pre_act * density)).astype(bf16)
    pre_ref[...] = grad_pre
    grad_rows = grad_ref[...].astype(f32)
    gate_grads = jnp.sum(act.astype(f32) * unscaled, axis=1, keepdims=True) + bias_dot_ref[...]
    gate_grads = jnp.broadcast_to(gate_grads, (gate_grads.shape[0], LANES)).T
    grad_y = (gate * grad_rows).astype(bf16)
    grady_ref[...] = grad_y

    @pl.when(pl.program_id(0) == 0)
    def _():
        dbin_ref[...] = jnp.zeros_like(dbin_ref)
        dbback_ref[...] = jnp.zeros_like(dbback_ref)

    ones = jnp.ones((8, grad_pre.shape[0]), bf16)
    dbin_ref[...] += dot(ones, grad_pre, 1, 0)[0:1, :]
    dbback_ref[...] += dot(ones, grad_y, 1, 0)[0:1, :]
    for key, piece_ref in enumerate(piece_refs):
        start = pl.multiple_of((tensor_id ^ key) * piece, LANES)
        rows = dot(grad_pre, w_in_ref[pl.ds(start, piece), :], 1, 1)
        for source in range(count):
            part = slice(source * capacity, (source + 1) * capacity)
            piece_ref[source, 0:capacity, :] = rows[part, :].astype(bf16)
            piece_ref[source, capacity : capacity + EXTRA, :] = jnp.zeros((EXTRA, piece), bf16)
            for first in range(0, capacity, piece):
                lanes = min(piece, capacity - first)
                place = capacity + first // piece
                here = source * capacity + first
                piece_ref[source, place : place + 1, 0:lanes] = gate_grads[
                    0:1, here : here + lanes
                ].astype(bf16)


def back_kernel(idx_ref, act_ref, gate_ref, w_ref, bias_ref, *piece_refs):
    blocks = len(piece_refs)
    piece = piece_refs[0].shape[-1]
    for key, piece_ref in enumerate(piece_refs):
        cols = pl.ds(pl.multiple_of((idx_ref[0] ^ key) * piece, LANES), piece)
        rows = dot(act_ref[...], w_ref[:, cols], 1, 0) + bias_ref[:, cols] * (1.0 / blocks)
        piece_ref[...] = (gate_ref[...] * rows).astype(bf16)


def outer_kernel(left_ref, right_ref, out_ref):
    out_ref[...] = dot(left_ref[...], right_ref[...], 0, 0)


def outer_halves_kernel(idx_ref, own_ref, other_ref, right_ref, out_ref):
    mine = (idx_ref[0] & 1) == pl.program_id(0) // 2

    @pl.when(mine)
    def _():
        out_ref[...] = dot(own_ref[...], right_ref[...], 0, 0)

    @pl.when(jnp.logical_not(mine))
    def _():
        out_ref[...] = dot(other_ref[...], right_ref[...], 0, 0)


def add_pairs_kernel(*refs):
    count = len(refs) // 3
    for left_ref, right_ref, out_ref in zip(refs[:count], refs[count : 2 * count], refs[2 * count :]):
        out_ref[...] = (left_ref[...].astype(f32) + right_ref[...].astype(f32)).astype(bf16)


def add_kernel(left_ref, right_ref, out_ref):
    out_ref[...] = (left_ref[...].astype(f32) + right_ref[...].astype(f32)).astype(bf16)


def combine_kernel(place_ref, home_ref, out_ref):
    out_ref[...] = dot(place_ref[...], home_ref[...], 1, 0).astype(bf16)


def finish_kernel(idx_ref, resid_ref, *refs):
    piece_refs, out_ref = refs[:-1], refs[-1]
    piece = piece_refs[0].shape[1]
    for key, piece_ref in enumerate(piece_refs):
        cols = pl.ds(pl.multiple_of((idx_ref[0] ^ key) * piece, LANES), piece)
        out_ref[:, cols] = (resid_ref[:, cols] + piece_ref[...].astype(f32)).astype(bf16)


def residual_kernel(*refs, blocks, capacity):
    idx_ref, piece_refs, refs = refs[0], refs[1 : 1 + blocks], refs[1 + blocks :]
    residual_body(idx_ref, piece_refs, *refs, capacity=capacity)


def residual_body(
    idx_ref,
    piece_refs,
    gg_ref,
    place_ref,
    probs_ref,
    second_ref,
    router_ref,
    resid_ref,
    gain_ref,
    dout_ref,
    w_ref,
    mix_ref,
    grad_ref,
    dw_keep_ref,
    dw_send_ref,
    gmix_ref,
    small_ref,
    disp_ref,
    *,
    capacity,
):
    probs = probs_ref[...]
    experts = probs.shape[1]
    slots = place_ref.shape[1]
    piece = piece_refs[0].shape[1]
    stride = capacity + EXTRA
    lane = lax.broadcasted_iota(jnp.int32, (experts, slots), 1)
    first = lax.broadcasted_iota(jnp.int32, (experts, slots), 0) * stride
    segment = (lane >= first) & (lane < first + capacity)
    gate_rows = jnp.where(segment, jnp.broadcast_to(gg_ref[...], (experts, slots)), 0.0)
    grad_probs = dot(place_ref[...], gate_rows.astype(bf16), 1, 1)
    for key, piece_ref in enumerate(piece_refs):
        cols = pl.ds(pl.multiple_of((idx_ref[0] ^ key) * piece, LANES), piece)
        disp_ref[:, cols] = piece_ref[...]
    grad_logits = (
        probs * (grad_probs - jnp.sum(probs * grad_probs, axis=1, keepdims=True))
    ).astype(bf16)
    second_grad = disp_ref[...].astype(f32) + dot(grad_logits, router_ref[...], 1, 1)
    normal, rstd = norm_parts(resid_ref[...])
    grad_resid = dout_ref[...].astype(f32) + norm_back(second_grad, normal, rstd, gain_ref[...])
    grad_ref[...] = grad_resid
    branch = grad_resid.astype(bf16)
    gmix_ref[...] = dot(branch, w_ref[...], 1, 1).astype(bf16)
    local = dw_keep_ref.shape[1]
    part = local // 2
    for ref, side in ((dw_keep_ref, idx_ref[4]), (dw_send_ref, 1 - idx_ref[4])):
        if part % LANES == 0:
            left = mix_ref[:, pl.ds(pl.multiple_of(side * part, LANES), part)]
        else:
            left = jnp.where(side == 0, mix_ref[:, 0:part], mix_ref[:, part:])
        product = dot(left, branch, 0, 0).astype(bf16)
        for block in range(product.shape[1] // local):
            ref[block * part : (block + 1) * part, :] = product[
                :, block * local : (block + 1) * local
            ]
    small_ref[0:experts, :] = dot(grad_logits, second_ref[...], 0, 0)
    small_ref[experts : experts + 1, :] = jnp.sum(second_grad * normal, axis=0, keepdims=True)
    small_ref[experts + 1 : experts + 2, :] = jnp.sum(second_grad, axis=0, keepdims=True)
    small_ref[experts + 2 : experts + 3, :] = jnp.sum(grad_resid, axis=0, keepdims=True)


def attend_back_kernel(
    idx_ref,
    q_ref,
    k_ref,
    v_ref,
    gmix_ref,
    norm_ref,
    w_ref,
    tok_ref,
    first_keep_ref,
    first_send_ref,
    second_keep_ref,
    second_send_ref,
    db_ref,
    part_keep_ref,
    part_send_ref,
    gq_ref,
    gk_ref,
    gv_ref,
    part_ref,
):
    rows = q_ref.shape[0]
    inside = same_image(rows)
    heads = lane_heads(rows)
    scale = HD ** (-0.5)
    for start in range(0, q_ref.shape[1], LANES):
        cols = slice(start, start + LANES)
        queries, keys, value_rows = q_ref[:, cols], k_ref[:, cols], v_ref[:, cols]
        grad_mixed = gmix_ref[:, cols]
        grad_q = jnp.zeros((rows, LANES), f32)
        grad_k = jnp.zeros((rows, LANES), f32)
        grad_v = jnp.zeros((rows, LANES), f32)
        for mask in heads:
            one_q = jnp.where(mask, queries, 0).astype(bf16)
            one_g = jnp.where(mask, grad_mixed, 0).astype(bf16)
            probs = head_probs(one_q, keys, inside)
            grad_v = grad_v + dot(probs.astype(bf16), one_g, 0, 0)
            grad_attn = dot(one_g, value_rows, 1, 1)
            delta = jnp.sum(probs * grad_attn, axis=-1, keepdims=True)
            grad_scores = (probs * (grad_attn - delta)).astype(bf16)
            grad_q = jnp.where(mask, dot(grad_scores, keys, 1, 0), grad_q)
            grad_k = grad_k + dot(grad_scores, one_q, 0, 0)
        gq_ref[:, cols] = (grad_q * scale).astype(bf16)
        gk_ref[:, cols] = (grad_k * scale).astype(bf16)
        gv_ref[:, cols] = grad_v.astype(bf16)
    quarter = norm_ref.shape[1] // 4
    total = None
    for part, ref in enumerate((gq_ref, gk_ref, gv_ref)):
        grads = ref[...]
        here = slice(part * quarter, (part + 1) * quarter)
        for side, base, keep_ref, send_ref in (
            (idx_ref[2], 0, first_keep_ref, first_send_ref),
            (idx_ref[3], 2, second_keep_ref, second_send_ref),
        ):
            for target, block in ((keep_ref, base + side), (send_ref, base + 1 - side)):
                cols = pl.ds(pl.multiple_of(block * quarter, LANES), quarter)
                target[here, :] = dot(norm_ref[:, cols], grads, 0, 0).astype(bf16)
        term = dot(grads, w_ref[part], 1, 1)
        total = term if total is None else total + term
    normal, _ = norm_parts(tok_ref[...].astype(f32))
    part_ref[0:rows, :] = total.astype(bf16)
    part_ref[rows:, :] = jnp.zeros((part_ref.shape[0] - rows, total.shape[1]), bf16)
    part_ref[rows : rows + 1, :] = jnp.sum(total * normal, axis=0, keepdims=True).astype(bf16)
    part_ref[rows + 1 : rows + 2, :] = jnp.sum(total, axis=0, keepdims=True).astype(bf16)
    half = part_keep_ref.shape[1]
    side = idx_ref[0] & 1
    part_keep_ref[...] = part_ref[:, pl.ds(pl.multiple_of(side * half, LANES), half)]
    part_send_ref[...] = part_ref[:, pl.ds(pl.multiple_of((1 - side) * half, LANES), half)]
    db_ref[0:1, :] = jnp.sum(gq_ref[...].astype(f32), axis=0, keepdims=True)
    db_ref[1:2, :] = jnp.sum(gv_ref[...].astype(f32), axis=0, keepdims=True)


def pack_kernel(idx_ref, mine_ref, theirs_ref, small_ref, bias_ref, out_ref, line_ref):
    lines, width = line_ref.shape
    local = out_ref.shape[1]
    half = width // 2
    side = idx_ref[0] & 1
    count = small_ref.shape[0]
    line_ref[...] = jnp.zeros_like(line_ref)
    line_ref[0:count, :] = small_ref[...]
    mine = pl.ds(pl.multiple_of(side * half, LANES), half)
    line_ref[count : count + 2, mine] = mine_ref[0:2, :].astype(f32)
    theirs = pl.ds(pl.multiple_of((1 - side) * half, LANES), half)
    line_ref[count : count + 2, theirs] = theirs_ref[0:2, :].astype(f32)
    line_ref[count + 2 : count + 4, 0:local] = bias_ref[...]
    for block in range(width // local):
        out_ref[block * lines : (block + 1) * lines, :] = line_ref[
            :, block * local : (block + 1) * local
        ].astype(bf16)


def first_kernel(idx_ref, tok_ref, gain_ref, mine_ref, theirs_ref, resid_ref, out_ref, grad_ref):
    rows, width = tok_ref.shape
    half = width // 2
    side = idx_ref[0] & 1
    grad_ref[:, pl.ds(pl.multiple_of(side * half, LANES), half)] = mine_ref[...]
    grad_ref[:, pl.ds(pl.multiple_of((1 - side) * half, LANES), half)] = theirs_ref[...]
    normal, rstd = norm_parts(tok_ref[...].astype(f32))
    grad = grad_ref[0:rows, :].astype(f32)
    out_ref[...] = resid_ref[...] + norm_back(grad, normal, rstd, gain_ref[...])


def assemble_kernel(idx_ref, *refs):
    out_ref = refs[-1]
    quarter = out_ref.shape[1] // 4
    for chunk in range(2):
        low = idx_ref[2 + chunk] == 0
        for part in range(3):
            rows = slice(part * quarter, (part + 1) * quarter)
            mine = refs[2 * chunk][rows, :].astype(f32)
            came = refs[2 * chunk + 1][rows, :].astype(f32)
            base = 2 * chunk * quarter
            out_ref[part, base : base + quarter, :] = jnp.where(low, mine, came)
            out_ref[part, base + quarter : base + 2 * quarter, :] = jnp.where(low, came, mine)


def assemble_out_kernel(idx_ref, mine_ref, came_ref, out_ref):
    local = out_ref.shape[0]
    part = local // 2
    low = idx_ref[4] == 0
    for block in range(out_ref.shape[1] // local):
        rows = slice(block * part, (block + 1) * part)
        cols = slice(block * local, (block + 1) * local)
        mine = mine_ref[rows, :].astype(f32)
        came = came_ref[rows, :].astype(f32)
        out_ref[0:part, cols] = jnp.where(low, mine, came)
        out_ref[part:, cols] = jnp.where(low, came, mine)


def on_device(
    tokens,
    gain_attn,
    shift_attn,
    w_qkv,
    b_qv,
    w_out,
    b_out,
    gain_moe,
    shift_moe,
    w_router,
    w_in,
    b_in,
    w_back,
    b_back,
    routes,
    d_out,
):
    groups = lax.axis_size("expert")
    blocks = lax.axis_size("tensor")
    rows, width = tokens.shape
    top = routes.shape[1]
    experts = w_router.shape[1]
    capacity = (top * rows * 16 // (10 * experts) + 7) // 8 * 8
    slots = experts * capacity
    local = w_qkv.shape[2]
    piece = width // blocks
    half = width // 2
    hidden = w_in.shape[2]
    row = lambda vec: vec.reshape(1, -1)
    tensor_id = lax.axis_index("tensor").astype(jnp.int32)
    expert_id = lax.axis_index("expert").astype(jnp.int32)
    chains = [chain_of(groups, masks) for masks in MASKS]
    ids = jnp.stack([tensor_id, expert_id] + [side_of(chain[0][1]) for chain in chains])
    stride = capacity + EXTRA
    row_bits = bits_of(blocks)

    dispatch_place, grad_send = call(
        functools.partial(route_kernel, experts=experts, capacity=capacity),
        [sds((slots, rows), bf16), sds((slots, piece), bf16)],
        [ids, routes.T, d_out],
        2.5,
        scalars=1,
    )
    w_out_all = gather_tensor(w_out, diagonal=True)
    tokens_in, grad_send = lax.optimization_barrier((tokens, grad_send))
    grad_came = lax.all_to_all(
        grad_send.reshape(experts, capacity, piece), "expert", 0, 0, tiled=True
    ).reshape(slots, piece)

    normed, queries, keys, value_rows, mixed = call(
        attend_kernel,
        [sds((rows, width), bf16)] + [sds((rows, local), bf16)] * 4,
        [tokens_in, row(gain_attn), row(shift_attn), w_qkv, b_qv],
        4.7,
    )
    mixed_all = gather_tensor(mixed)
    residual, second_low, router_probs, send = call(
        functools.partial(middle_kernel, blocks=blocks),
        [
            sds((rows, width), f32),
            sds((rows, width), bf16),
            sds((rows, experts), f32),
            sds((slots, half), bf16),
        ],
        [
            ids,
            *mixed_all,
            *w_out_all,
            tokens,
            row(b_out),
            row(gain_moe),
            row(shift_moe),
            w_router,
            dispatch_place,
        ],
        5.5,
        scalars=1,
        scratch=[pltpu.VMEM((blocks, rows, width), f32)],
    )

    plain, padded = call(
        functools.partial(place_kernel, experts=experts, capacity=capacity),
        [sds((rows, slots), bf16), sds((rows, experts * stride), bf16)],
        [routes],
        2.5,
        after=[send],
    )

    own = lax.all_to_all(
        send.reshape(experts, capacity, half), "expert", 0, 0, tiled=True
    ).reshape(slots, half)
    smem = pl.BlockSpec(memory_space=pltpu.SMEM)
    count = max(1, min(experts, 320 // capacity))
    tile = count * capacity
    steps = slots // tile

    def whole(shape):
        return pl.BlockSpec(shape, lambda i: (0,) * len(shape))

    def by_row(cols):
        return pl.BlockSpec((tile, cols), lambda i: (i, 0))

    grad_rows, unscaled, bias_dot = call(
        functools.partial(early_kernel, blocks=blocks),
        [sds((slots, width), bf16), sds((slots, hidden), f32), sds((slots, 1), f32)],
        [ids, *gather_tensor(grad_came, diagonal=True), w_back[0], b_back],
        7.0,
        grid=(steps,),
        in_specs=[smem] + [by_row(piece)] * blocks + [whole((hidden, width)), whole((1, width))],
        out_specs=[by_row(width), by_row(hidden), by_row(1)],
    )
    own, grad_rows, unscaled = lax.optimization_barrier((own, grad_rows, unscaled))
    other = swap(own, "tensor", 1)

    outs = call(
        functools.partial(expert_kernel, blocks=blocks),
        [sds((experts, stride, piece), bf16)] * blocks
        + [
            sds((slots, hidden), bf16),
            sds((slots, hidden), bf16),
            sds((slots, width), bf16),
            sds((slots, 1), f32),
            sds((1, hidden), f32),
            sds((1, width), f32),
        ],
        [ids, own, other, grad_rows, unscaled, bias_dot, w_in[0], b_in, w_router],
        17.0,
        grid=(steps,),
        in_specs=[
            smem,
            by_row(half),
            by_row(half),
            by_row(width),
            by_row(hidden),
            by_row(1),
            whole((width, hidden)),
            whole((1, hidden)),
            whole((width, experts)),
        ],
        out_specs=[pl.BlockSpec((count, stride, piece), lambda i: (i, 0, 0))] * blocks
        + [
            by_row(hidden),
            by_row(hidden),
            by_row(width),
            by_row(1),
            whole((1, hidden)),
            whole((1, width)),
        ],
    )
    held = scatter_step(dict(enumerate(outs[:blocks])), row_bits[0])
    activated, grad_pre, grad_y, gate, d_b_in, d_b_back = outs[blocks:]
    held, activated, grad_pre, grad_y = lax.optimization_barrier(
        (held, activated, grad_pre, grad_y)
    )

    out_pieces = call(
        back_kernel,
        [sds((slots, piece), bf16)] * blocks,
        [ids, activated, gate, w_back[0], b_back],
        6.5,
        grid=(steps,),
        in_specs=[smem, by_row(hidden), by_row(1), whole((hidden, width)), whole((1, width))],
        out_specs=[by_row(piece)] * blocks,
    )
    kept = [key for key in range(blocks) if not key & 1]
    out_came = [swap(out_pieces[key | 1], "tensor", 1) for key in kept]

    for bit in row_bits[1:]:
        held = scatter_step(held, bit)
    home = lax.all_to_all(held[0], "expert", 0, 0, tiled=True)
    out_sums = call(
        add_pairs_kernel,
        [sds((slots, piece), bf16)] * len(kept),
        [out_pieces[key] for key in kept] + out_came,
        2.0,
        grid=(steps,),
        in_specs=[by_row(piece)] * (2 * len(kept)),
        out_specs=[by_row(piece)] * len(kept),
        after=[held[0]],
    )
    out_held = scatter_sent(dict(zip(kept, out_sums)), row_bits)

    cut = min(256, hidden)
    d_w_back = call(
        outer_kernel,
        [sds((hidden, width), f32)],
        [activated, grad_y],
        7.0,
        grid=(hidden // cut,),
        in_specs=[pl.BlockSpec((slots, cut), lambda i: (0, i)), whole((slots, width))],
        out_specs=[pl.BlockSpec((cut, width), lambda i: (i, 0))],
        after=out_sums,
    )[0][None]
    d_w_in = call(
        outer_halves_kernel,
        [sds((width, hidden), f32)],
        [ids, own, other, grad_pre],
        7.0,
        grid=(4,),
        in_specs=[
            smem,
            pl.BlockSpec((slots, half // 2), lambda i: (0, i % 2)),
            pl.BlockSpec((slots, half // 2), lambda i: (0, i % 2)),
            whole((slots, hidden)),
        ],
        out_specs=[pl.BlockSpec((half // 2, hidden), lambda i: (i, 0))],
        after=out_sums,
    )[0][None]
    dispatch = call(
        combine_kernel,
        [sds((rows, piece), bf16)],
        [padded, home.reshape(experts * stride, piece)],
        1.8,
        after=[d_w_back, d_w_in],
    )[0]
    dispatch_all = gather_tensor(dispatch)
    gate_lines = -(-capacity // piece)
    gate_grads = home[:, capacity : capacity + gate_lines, :].reshape(experts, gate_lines * piece)
    gate_grads = jnp.pad(gate_grads[:, :capacity].astype(f32), ((0, 0), (0, EXTRA)))
    gate_grads = gate_grads.reshape(1, experts * stride)

    out_sent = scatter_last(out_held, row_bits)

    out_home = lax.all_to_all(
        out_sent.reshape(experts, capacity, piece), "expert", 0, 0, tiled=True
    ).reshape(slots, piece)
    mixture = call(
        combine_kernel, [sds((rows, piece), bf16)], [plain, out_home], 1.8    )[0]
    activations = call(
        finish_kernel,
        [sds((rows, width), bf16)],
        [ids, residual, *gather_tensor(mixture)],
        2.6,
        scalars=1,
    )[0]

    grad_resid, out_keep, out_give, grad_mixed, small = call(
        functools.partial(residual_kernel, blocks=blocks, capacity=capacity),
        [
            sds((rows, width), f32),
            sds((half, local), bf16),
            sds((half, local), bf16),
            sds((rows, local), bf16),
            sds((experts + 3, width), f32),
        ],
        [
            ids,
            *dispatch_all,
            gate_grads,
            padded,
            router_probs,
            second_low,
            w_router,
            residual,
            row(gain_moe),
            d_out,
            w_out,
            mixed,
        ],
        6.0,
        scalars=1,
        scratch=[pltpu.VMEM((rows, width), bf16)],
    )
    out_came = swap(out_give, "expert", chains[2][0][0])
    quarter = width // 4
    padded_rows = -(-(rows + 2) // EXTRA) * EXTRA
    outs = call(
        attend_back_kernel,
        [sds((3 * quarter, local), bf16)] * 4
        + [
            sds((2, local), f32),
            sds((padded_rows, half), bf16),
            sds((padded_rows, half), bf16),
            sds((rows, local), bf16),
            sds((rows, local), bf16),
            sds((rows, local), bf16),
        ],
        [ids, queries, keys, value_rows, grad_mixed, normed, w_qkv, tokens],
        8.0,
        scalars=1,
        scratch=[pltpu.VMEM((padded_rows, width), bf16)],
    )
    first_came = swap(outs[1], "expert", chains[0][0][0])
    second_came = swap(outs[3], "expert", chains[1][0][0])
    d_b_qv, part_keep, part_send = outs[4:7]

    mine = add(part_keep, swap(part_send, "tensor", 1))
    part_sum = mine
    for bit in row_bits[1:]:
        mine = add(mine, swap(mine, "tensor", bit))
    theirs = swap(mine, "tensor", 1)
    theirs = swap(mine, "tensor", 1)
    lines = -(-(experts + 7) // EXTRA) * EXTRA
    packed = call(
        pack_kernel,
        [sds((lines * (width // local), local), bf16)],
        [ids, mine[rows:], theirs[rows:], small, d_b_qv],
        1.0,
        scalars=1,
        scratch=[pltpu.VMEM((lines, width), f32)],
    )[0]
    first_sum = call(
        add_kernel, [sds(first_came.shape, bf16)], [outs[0], first_came], 0.8, after=[part_sum]
    )[0]
    first_sums = reduce_experts(first_sum, chains[0])
    second_sums = reduce_experts(add(outs[2], second_came), chains[1])
    out_sum = call(
        add_kernel,
        [sds(out_keep.shape, bf16)],
        [out_keep, out_came],
        0.8,
        after=[second_came],
    )[0]
    out_sums = reduce_experts(out_sum, chains[2])
    *first, packed = spread_experts(first_sums[-1], chains[0], packed)
    second = spread_experts(second_sums[-1], chains[1])[:2]
    d_w_out = spread_experts(out_sums[-1], chains[2])[:2]
    packed = packed.reshape(width // local, lines, local).transpose(1, 0, 2)
    packed = packed.reshape(lines, width).astype(f32)

    d_tokens = call(
        first_kernel,
        [sds((rows, width), f32)],
        [ids, tokens, row(gain_attn), mine, theirs, grad_resid],
        3.9,
        scalars=1,
        scratch=[pltpu.VMEM((padded_rows, width), bf16)],
    )[0]
    d_w_qkv = call(
        assemble_kernel,
        [sds((3, width, local), f32)],
        [ids, *first, *second],
        2.0,
        scalars=1,
        after=[d_tokens],
    )[0]
    d_w_out = call(
        assemble_out_kernel,
        [sds((local, width), f32)],
        [ids, *d_w_out],
        1.0,
        scalars=1,
    )[0]
    return (
        activations,
        d_tokens,
        packed[experts + 3],
        packed[experts + 4],
        d_w_qkv,
        packed[experts + 5 : experts + 7, :local],
        d_w_out,
        packed[experts + 2],
        packed[experts],
        packed[experts + 1],
        packed[:experts].T,
        d_w_in,
        d_b_in,
        d_w_back,
        d_b_back,
    )


def solution(mesh):
    in_specs = (
        P("expert", None),
        P(),
        P(),
        P(None, None, "tensor"),
        P(None, "tensor"),
        P("tensor", None),
        P(),
        P(),
        P(),
        P(),
        P("expert", None, "tensor"),
        P("expert", "tensor"),
        P("expert", "tensor", None),
        P("expert", None),
        P("expert", None),
        P("expert", None),
    )
    out_specs = (
        P("expert", None),
        P("expert", None),
        P(),
        P(),
        P(None, None, "tensor"),
        P(None, "tensor"),
        P("tensor", None),
        P(),
        P(),
        P(),
        P(),
        P("expert", None, "tensor"),
        P("expert", "tensor"),
        P("expert", "tensor", None),
        P("expert", None),
    )
    return jax.shard_map(
        on_device, mesh=mesh, in_specs=in_specs, out_specs=out_specs, check_vma=False
    )
```

```python
import functools

import jax
import jax.numpy as jnp
from jax import lax
from jax.experimental import pallas as pl
from jax.experimental.pallas import tpu as pltpu
from jax.sharding import PartitionSpec as P

HD = 64
SEQ = 197
LANES = 128
VMEM_LIMIT = 52 * 1024 * 1024
EXTRA = 16
MASKS = ((1, 2, 4), (2, 1, 5), (1, 3, 6))
FLOPS_PER_US = 1.15e9

epsilon = 1e-06
f32 = jnp.float32
bf16 = jnp.bfloat16


def dot(left, right, left_dim, right_dim, precision=None):
    return lax.dot_general(
        left,
        right,
        (((left_dim,), (right_dim,)), ((), ())),
        precision=precision,
        preferred_element_type=f32,
    )


def call(
    body, outs, ins, us, grid=None, in_specs=None, out_specs=None, scalars=0, scratch=(), after=()
):
    specs = {"scratch_shapes": list(scratch)}
    if grid is not None:
        specs["grid"] = grid
        specs["out_specs"] = out_specs
    else:
        in_specs = [
            pl.BlockSpec(memory_space=pltpu.SMEM if i < scalars else pltpu.VMEM)
            for i in range(len(ins))
        ]
        specs["out_specs"] = [pl.BlockSpec(memory_space=pltpu.VMEM) for _ in outs]
    specs["in_specs"] = in_specs + [pl.BlockSpec(memory_space=pl.ANY)] * len(after)
    used = len(ins)

    def run(*refs):
        body(*refs[:used], *refs[used + len(after) :])

    return pl.pallas_call(
        run,
        out_shape=outs,
        compiler_params=pltpu.CompilerParams(vmem_limit_bytes=VMEM_LIMIT),
        cost_estimate=pl.CostEstimate(
            flops=int(us * FLOPS_PER_US), bytes_accessed=0, transcendentals=0
        ),
        **specs,
    )(*ins, *after)


def sds(shape, dtype):
    return jax.ShapeDtypeStruct(shape, dtype)


def swap(values, axis, bit):
    count = lax.axis_size(axis)
    return lax.ppermute(values, axis, [(i, i ^ bit) for i in range(count)])


def bits_of(count):
    return [1 << i for i in range(count.bit_length() - 1)]


def gather_tensor(values, diagonal=False):
    count = lax.axis_size("tensor")
    held = {0: values}
    for bit in reversed(bits_of(count)):
        step = bit ^ 1 if diagonal and bit > 1 else bit
        for key in list(held):
            held[key ^ step] = swap(held[key], "tensor", step)
    return [held[key] for key in range(count)]


def add(left, right):
    return (left.astype(f32) + right.astype(f32)).astype(left.dtype)


def scatter_step(held, bit):
    kept = {}
    for key in sorted(held):
        if not key & bit:
            kept[key] = add(held[key], swap(held[key | bit], "tensor", bit))
    return kept


def scatter_sent(held, bits):
    for bit in bits[1:-1]:
        held = scatter_step(held, bit)
    if len(bits) == 1:
        return held
    return {0: held[0], 1: swap(held[bits[-1]], "tensor", bits[-1])}


def scatter_last(held, bits):
    return held[0] if len(bits) == 1 else add(held[0], held[1])


def butterfly(values, axis):
    for bit in bits_of(lax.axis_size(axis)):
        came = swap(values, axis, bit)
        values = add(values, came)
    return values


def chain_of(count, masks):
    masks = [m for m in masks if m < count]
    masks += bits_of(count)[len(masks) :]
    parity = lambda value: bin(value).count("1") % 2
    sides = []
    for step in range(len(masks)):
        wanted = [int(step == other) for other in range(len(masks))]
        fits = [d for d in range(count) if [parity(d & m) for m in masks] == wanted]
        sides.append(fits[0])
    return list(zip(masks, sides))


def side_of(bits):
    index = lax.axis_index("expert")
    total = sum(((index >> b) & 1 for b in range(bits.bit_length()) if (bits >> b) & 1))
    return (total & 1).astype(jnp.int32)


def reduce_experts(values, chain):
    sums = [values]
    for mask, bits in chain[1:]:
        half = values.shape[0] // 2
        side = side_of(bits)
        keep = lax.dynamic_slice_in_dim(values, side * half, half, 0)
        send = lax.dynamic_slice_in_dim(values, (1 - side) * half, half, 0)
        values = add(keep, swap(send, "expert", mask))
        sums.append(values)
    return sums


def spread_experts(values, chain, rider=None):
    count = 0 if rider is None else rider.shape[0]
    for mask, bits in reversed(chain):
        rows = values.shape[0]
        sent = values if rider is None else jnp.concatenate([values, rider], 0)
        came = swap(sent, "expert", mask)
        if rider is not None:
            rider = add(rider, came[rows : rows + count])
        came = came[:rows]
        if (mask, bits) == chain[0]:
            return values, came, rider
        values = jnp.where(
            side_of(bits) == 0,
            jnp.concatenate([values, came], 0),
            jnp.concatenate([came, values], 0),
        )


def norm_parts(values):
    center = values - jnp.mean(values, axis=-1, keepdims=True)
    variance = jnp.mean(center * center, axis=-1, keepdims=True)
    rstd = lax.rsqrt(variance + epsilon)
    return center * rstd, rstd


def norm_back(grad, normal, rstd, gain):
    scaled = grad * gain
    mean_g = jnp.mean(scaled, axis=-1, keepdims=True)
    mean_gn = jnp.mean(scaled * normal, axis=-1, keepdims=True)
    return rstd * (scaled - mean_g - normal * mean_gn)


def same_image(rows):
    left = lax.broadcasted_iota(jnp.int32, (rows, rows), 0)
    right = lax.broadcasted_iota(jnp.int32, (rows, rows), 1)
    left_id = jnp.zeros((rows, rows), jnp.int32)
    right_id = jnp.zeros((rows, rows), jnp.int32)
    for edge in range(SEQ, rows, SEQ):
        left_id = left_id + (left >= edge).astype(jnp.int32)
        right_id = right_id + (right >= edge).astype(jnp.int32)
    return left_id == right_id


def head_probs(queries, keys, inside):
    scores = dot(queries, keys, 1, 1) * (HD ** (-0.5))
    scores = jnp.where(inside, scores, -1e30)
    top = jnp.max(scores, axis=-1, keepdims=True)
    powers = jnp.exp(scores - top)
    return powers * (1.0 / jnp.sum(powers, axis=-1, keepdims=True))


def lane_heads(rows):
    lane = lax.broadcasted_iota(jnp.int32, (rows, LANES), 1)
    return [(lane // HD) == head for head in range(LANES // HD)]


def attend_kernel(tok_ref, gain_ref, shift_ref, w_ref, b_ref, norm_ref, q_ref, k_ref, v_ref, mix_ref):
    rows = tok_ref.shape[0]
    normal, _ = norm_parts(tok_ref[...].astype(f32))
    normed = (normal * gain_ref[...] + shift_ref[...]).astype(bf16)
    norm_ref[...] = normed
    q_ref[...] = (dot(normed, w_ref[0], 1, 0) + b_ref[0:1, :]).astype(bf16)
    k_ref[...] = dot(normed, w_ref[1], 1, 0).astype(bf16)
    v_ref[...] = (dot(normed, w_ref[2], 1, 0) + b_ref[1:2, :]).astype(bf16)
    inside = same_image(rows)
    heads = lane_heads(rows)
    for start in range(0, q_ref.shape[1], LANES):
        cols = slice(start, start + LANES)
        queries, keys, value_rows = q_ref[:, cols], k_ref[:, cols], v_ref[:, cols]
        mixed = jnp.zeros((rows, LANES), f32)
        for mask in heads:
            probs = head_probs(jnp.where(mask, queries, 0).astype(bf16), keys, inside)
            mixed = jnp.where(mask, dot(probs.astype(bf16), value_rows, 1, 0), mixed)
        mix_ref[:, cols] = mixed.astype(bf16)


def slot_numbers(named, earlier, ids, axis, stride):
    numbers = []
    for mask in named:
        slot = jnp.sum(jnp.where(mask, earlier, 0.0), axis=axis, keepdims=True).astype(jnp.int32)
        owner = jnp.sum(jnp.where(mask, ids, 0), axis=axis, keepdims=True)
        numbers.append(owner * stride + slot)
    return numbers


def one_hot(targets, shape, axis):
    ids = lax.broadcasted_iota(jnp.int32, shape, axis)
    table = jnp.zeros(shape, f32)
    for target in targets:
        table = jnp.where(ids == target, 1.0, table)
    return table.astype(bf16)


def route_kernel(
    idx_ref,
    routes_ref,
    flipped_ref,
    dout_ref,
    plain_ref,
    padded_ref,
    dispatch_ref,
    send_ref,
    *,
    experts,
    capacity,
):
    place_kernel(routes_ref, plain_ref, padded_ref, experts=experts, capacity=capacity)
    rows = dispatch_ref.shape[1]
    width = send_ref.shape[1]
    first = lax.broadcasted_iota(jnp.int32, (rows, rows), 0)
    second = lax.broadcasted_iota(jnp.int32, (rows, rows), 1)
    ids = lax.broadcasted_iota(jnp.int32, (experts, rows), 0)
    named = [flipped_ref[k : k + 1, :] == ids for k in range(flipped_ref.shape[0])]
    tally = sum(m.astype(f32) for m in named).astype(bf16)
    earlier = dot(tally, (first < second).astype(f32).astype(bf16), 1, 0)
    numbers = slot_numbers(named, earlier, ids, 0, capacity)
    dispatch_ref[...] = one_hot(numbers, dispatch_ref.shape, 0)
    start = pl.multiple_of(idx_ref[0] * width, LANES)
    send_ref[...] = dot(dispatch_ref[...], dout_ref[:, pl.ds(start, width)], 1, 0).astype(bf16)


def place_kernel(routes_ref, plain_ref, padded_ref, *, experts, capacity):
    rows = plain_ref.shape[0]
    first = lax.broadcasted_iota(jnp.int32, (rows, rows), 0)
    second = lax.broadcasted_iota(jnp.int32, (rows, rows), 1)
    ids = lax.broadcasted_iota(jnp.int32, (rows, experts), 1)
    named = [routes_ref[:, k : k + 1] == ids for k in range(routes_ref.shape[1])]
    tally = sum(m.astype(f32) for m in named).astype(bf16)
    earlier = dot((second < first).astype(f32).astype(bf16), tally, 1, 0)
    for ref, stride in ((plain_ref, capacity), (padded_ref, capacity + EXTRA)):
        ref[...] = one_hot(slot_numbers(named, earlier, ids, 1, stride), ref.shape, 1)


def middle_kernel(*refs, blocks):
    idx_ref, refs = refs[0], refs[1:]
    mix_refs, w_refs, refs = refs[:blocks], refs[blocks : 2 * blocks], refs[2 * blocks :]
    tok_ref, bias_ref, gain_ref, shift_ref, router_ref, dispatch_ref = refs[:6]
    resid_ref, second_ref, probs_ref, send_ref, terms_ref = refs[6:]
    width = send_ref.shape[1]
    for key in range(blocks):
        terms_ref[key] = dot(mix_refs[key][...], w_refs[key][...], 1, 0)
    terms = [terms_ref[key] for key in range(blocks)]
    while len(terms) > 1:
        terms = [terms[i] + terms[i + 1] for i in range(0, len(terms), 2)]
    residual = tok_ref[...].astype(f32) + terms[0] + bias_ref[...]
    resid_ref[...] = residual
    normal, _ = norm_parts(residual)
    second_ref[...] = (normal * gain_ref[...] + shift_ref[...]).astype(bf16)
    start = pl.multiple_of((idx_ref[0] & 1) * width, LANES)
    send_ref[...] = dot(dispatch_ref[...], second_ref[:, pl.ds(start, width)], 1, 0).astype(bf16)
    logits = dot(second_ref[...], router_ref[...], 1, 0)
    powers = jnp.exp(logits - jnp.max(logits, axis=-1, keepdims=True))
    probs_ref[...] = powers / jnp.sum(powers, axis=-1, keepdims=True)


def early_kernel(*refs, blocks):
    idx_ref, piece_refs = refs[0], refs[1 : 1 + blocks]
    w_ref, bias_ref, rows_ref, unscaled_ref, bias_dot_ref = refs[1 + blocks :]
    piece = piece_refs[0].shape[-1]
    for key, piece_ref in enumerate(piece_refs):
        cols = pl.ds(pl.multiple_of((idx_ref[0] ^ key) * piece, LANES), piece)
        rows_ref[:, cols] = piece_ref[...]
    unscaled_ref[...] = dot(rows_ref[...], w_ref[...], 1, 1)
    bias_dot_ref[...] = jnp.sum(
        rows_ref[...].astype(f32) * bias_ref[...], axis=1, keepdims=True
    ) * (1.0 / blocks)


def expert_kernel(
    idx_ref,
    own_ref,
    other_ref,
    grad_ref,
    unscaled_ref,
    bias_dot_ref,
    w_in_ref,
    b_in_ref,
    router_ref,
    *outs,
    blocks,
):
    piece_refs = outs[:blocks]
    act_ref, pre_ref, grady_ref, gate_ref, dbin_ref, dbback_ref = outs[blocks:]
    count, capacity = piece_refs[0].shape[0], piece_refs[0].shape[1] - EXTRA
    tensor_id, expert_id = idx_ref[0], idx_ref[1]
    side = tensor_id & 1
    width = w_in_ref.shape[0] // 2
    piece = w_in_ref.shape[0] // blocks
    own, other = own_ref[...], other_ref[...]
    low_half = jnp.where(side == 0, own, other)
    high_half = jnp.where(side == 0, other, own)
    logits = dot(low_half, router_ref[0:width, :], 1, 0) + dot(
        high_half, router_ref[width:, :], 1, 0
    )
    powers = jnp.exp(logits - jnp.max(logits, axis=-1, keepdims=True))
    ids = lax.broadcasted_iota(jnp.int32, logits.shape, 1)
    gate = jnp.sum(jnp.where(ids == expert_id, powers, 0.0), axis=-1, keepdims=True) / jnp.sum(
        powers, axis=-1, keepdims=True
    )
    gate_ref[...] = gate
    pre_act = (
        dot(low_half, w_in_ref[0:width, :], 1, 0)
        + dot(high_half, w_in_ref[width:, :], 1, 0)
        + b_in_ref[...]
    )
    cdf = 0.5 * (1.0 + lax.erf(pre_act * (2.0**-0.5)))
    density = jnp.exp(-0.5 * pre_act * pre_act) * 0.3989422804014327
    act = (pre_act * cdf).astype(bf16)
    act_ref[...] = act
    unscaled = unscaled_ref[...]
    grad_pre = (gate * unscaled * (cdf + pre_act * density)).astype(bf16)
    pre_ref[...] = grad_pre
    grad_rows = grad_ref[...].astype(f32)
    gate_grads = jnp.sum(act.astype(f32) * unscaled, axis=1, keepdims=True) + bias_dot_ref[...]
    gate_grads = jnp.broadcast_to(gate_grads, (gate_grads.shape[0], LANES)).T
    grad_y = (gate * grad_rows).astype(bf16)
    grady_ref[...] = grad_y

    @pl.when(pl.program_id(0) == 0)
    def _():
        dbin_ref[...] = jnp.zeros_like(dbin_ref)
        dbback_ref[...] = jnp.zeros_like(dbback_ref)

    ones = jnp.ones((8, grad_pre.shape[0]), bf16)
    dbin_ref[...] += dot(ones, grad_pre, 1, 0)[0:1, :]
    dbback_ref[...] += dot(ones, grad_y, 1, 0)[0:1, :]
    for key, piece_ref in enumerate(piece_refs):
        start = pl.multiple_of((tensor_id ^ key) * piece, LANES)
        rows = dot(grad_pre, w_in_ref[pl.ds(start, piece), :], 1, 1)
        for source in range(count):
            part = slice(source * capacity, (source + 1) * capacity)
            piece_ref[source, 0:capacity, :] = rows[part, :].astype(bf16)
            piece_ref[source, capacity : capacity + EXTRA, :] = jnp.zeros((EXTRA, piece), bf16)
            for first in range(0, capacity, piece):
                lanes = min(piece, capacity - first)
                place = capacity + first // piece
                here = source * capacity + first
                piece_ref[source, place : place + 1, 0:lanes] = gate_grads[
                    0:1, here : here + lanes
                ].astype(bf16)


def back_kernel(idx_ref, act_ref, gate_ref, w_ref, bias_ref, *piece_refs):
    blocks = len(piece_refs)
    piece = piece_refs[0].shape[-1]
    for key, piece_ref in enumerate(piece_refs):
        cols = pl.ds(pl.multiple_of((idx_ref[0] ^ key) * piece, LANES), piece)
        rows = dot(act_ref[...], w_ref[:, cols], 1, 0) + bias_ref[:, cols] * (1.0 / blocks)
        piece_ref[...] = (gate_ref[...] * rows).astype(bf16)


def outer_kernel(left_ref, right_ref, out_ref):
    out_ref[...] = dot(left_ref[...], right_ref[...], 0, 0)


def outer_halves_kernel(idx_ref, own_ref, other_ref, right_ref, out_ref):
    mine = (idx_ref[0] & 1) == pl.program_id(0) // 2

    @pl.when(mine)
    def _():
        out_ref[...] = dot(own_ref[...], right_ref[...], 0, 0)

    @pl.when(jnp.logical_not(mine))
    def _():
        out_ref[...] = dot(other_ref[...], right_ref[...], 0, 0)


def add_pairs_kernel(*refs):
    count = len(refs) // 3
    for left_ref, right_ref, out_ref in zip(refs[:count], refs[count : 2 * count], refs[2 * count :]):
        out_ref[...] = (left_ref[...].astype(f32) + right_ref[...].astype(f32)).astype(bf16)


def add_kernel(left_ref, right_ref, out_ref):
    out_ref[...] = (left_ref[...].astype(f32) + right_ref[...].astype(f32)).astype(bf16)


def combine_kernel(place_ref, home_ref, out_ref):
    out_ref[...] = dot(place_ref[...], home_ref[...], 1, 0).astype(bf16)


def finish_kernel(idx_ref, resid_ref, *refs):
    piece_refs, out_ref = refs[:-1], refs[-1]
    piece = piece_refs[0].shape[1]
    for key, piece_ref in enumerate(piece_refs):
        cols = pl.ds(pl.multiple_of((idx_ref[0] ^ key) * piece, LANES), piece)
        out_ref[:, cols] = (resid_ref[:, cols] + piece_ref[...].astype(f32)).astype(bf16)


def residual_kernel(*refs, blocks, capacity):
    idx_ref, piece_refs, refs = refs[0], refs[1 : 1 + blocks], refs[1 + blocks :]
    residual_body(idx_ref, piece_refs, *refs, capacity=capacity)


def residual_body(
    idx_ref,
    piece_refs,
    gg_ref,
    place_ref,
    probs_ref,
    second_ref,
    router_ref,
    resid_ref,
    gain_ref,
    dout_ref,
    w_ref,
    mix_ref,
    grad_ref,
    dw_keep_ref,
    dw_send_ref,
    gmix_ref,
    small_ref,
    disp_ref,
    *,
    capacity,
):
    probs = probs_ref[...]
    experts = probs.shape[1]
    slots = place_ref.shape[1]
    piece = piece_refs[0].shape[1]
    stride = capacity + EXTRA
    lane = lax.broadcasted_iota(jnp.int32, (experts, slots), 1)
    first = lax.broadcasted_iota(jnp.int32, (experts, slots), 0) * stride
    segment = (lane >= first) & (lane < first + capacity)
    gate_rows = jnp.where(segment, jnp.broadcast_to(gg_ref[...], (experts, slots)), 0.0)
    grad_probs = dot(place_ref[...], gate_rows.astype(bf16), 1, 1)
    for key, piece_ref in enumerate(piece_refs):
        cols = pl.ds(pl.multiple_of((idx_ref[0] ^ key) * piece, LANES), piece)
        disp_ref[:, cols] = piece_ref[...]
    grad_logits = (
        probs * (grad_probs - jnp.sum(probs * grad_probs, axis=1, keepdims=True))
    ).astype(bf16)
    second_grad = disp_ref[...].astype(f32) + dot(grad_logits, router_ref[...], 1, 1)
    normal, rstd = norm_parts(resid_ref[...])
    grad_resid = dout_ref[...].astype(f32) + norm_back(second_grad, normal, rstd, gain_ref[...])
    grad_ref[...] = grad_resid
    branch = grad_resid.astype(bf16)
    gmix_ref[...] = dot(branch, w_ref[...], 1, 1).astype(bf16)
    local = dw_keep_ref.shape[1]
    part = local // 2
    for ref, side in ((dw_keep_ref, idx_ref[4]), (dw_send_ref, 1 - idx_ref[4])):
        if part % LANES == 0:
            left = mix_ref[:, pl.ds(pl.multiple_of(side * part, LANES), part)]
        else:
            left = jnp.where(side == 0, mix_ref[:, 0:part], mix_ref[:, part:])
        product = dot(left, branch, 0, 0).astype(bf16)
        for block in range(product.shape[1] // local):
            ref[block * part : (block + 1) * part, :] = product[
                :, block * local : (block + 1) * local
            ]
    small_ref[0:experts, :] = dot(grad_logits, second_ref[...], 0, 0)
    small_ref[experts : experts + 1, :] = jnp.sum(second_grad * normal, axis=0, keepdims=True)
    small_ref[experts + 1 : experts + 2, :] = jnp.sum(second_grad, axis=0, keepdims=True)
    small_ref[experts + 2 : experts + 3, :] = jnp.sum(grad_resid, axis=0, keepdims=True)


def attend_back_kernel(
    idx_ref,
    q_ref,
    k_ref,
    v_ref,
    gmix_ref,
    norm_ref,
    w_ref,
    tok_ref,
    first_keep_ref,
    first_send_ref,
    second_keep_ref,
    second_send_ref,
    db_ref,
    part_keep_ref,
    part_send_ref,
    gq_ref,
    gk_ref,
    gv_ref,
    part_ref,
):
    rows = q_ref.shape[0]
    inside = same_image(rows)
    heads = lane_heads(rows)
    scale = HD ** (-0.5)
    for start in range(0, q_ref.shape[1], LANES):
        cols = slice(start, start + LANES)
        queries, keys, value_rows = q_ref[:, cols], k_ref[:, cols], v_ref[:, cols]
        grad_mixed = gmix_ref[:, cols]
        grad_q = jnp.zeros((rows, LANES), f32)
        grad_k = jnp.zeros((rows, LANES), f32)
        grad_v = jnp.zeros((rows, LANES), f32)
        for mask in heads:
            one_q = jnp.where(mask, queries, 0).astype(bf16)
            one_g = jnp.where(mask, grad_mixed, 0).astype(bf16)
            probs = head_probs(one_q, keys, inside)
            grad_v = grad_v + dot(probs.astype(bf16), one_g, 0, 0)
            grad_attn = dot(one_g, value_rows, 1, 1)
            delta = jnp.sum(probs * grad_attn, axis=-1, keepdims=True)
            grad_scores = (probs * (grad_attn - delta)).astype(bf16)
            grad_q = jnp.where(mask, dot(grad_scores, keys, 1, 0), grad_q)
            grad_k = grad_k + dot(grad_scores, one_q, 0, 0)
        gq_ref[:, cols] = (grad_q * scale).astype(bf16)
        gk_ref[:, cols] = (grad_k * scale).astype(bf16)
        gv_ref[:, cols] = grad_v.astype(bf16)
    quarter = norm_ref.shape[1] // 4
    total = None
    for part, ref in enumerate((gq_ref, gk_ref, gv_ref)):
        grads = ref[...]
        here = slice(part * quarter, (part + 1) * quarter)
        for side, base, keep_ref, send_ref in (
            (idx_ref[2], 0, first_keep_ref, first_send_ref),
            (idx_ref[3], 2, second_keep_ref, second_send_ref),
        ):
            for target, block in ((keep_ref, base + side), (send_ref, base + 1 - side)):
                cols = pl.ds(pl.multiple_of(block * quarter, LANES), quarter)
                target[here, :] = dot(norm_ref[:, cols], grads, 0, 0).astype(bf16)
        term = dot(grads, w_ref[part], 1, 1)
        total = term if total is None else total + term
    normal, _ = norm_parts(tok_ref[...].astype(f32))
    part_ref[0:rows, :] = total.astype(bf16)
    part_ref[rows:, :] = jnp.zeros((part_ref.shape[0] - rows, total.shape[1]), bf16)
    part_ref[rows : rows + 1, :] = jnp.sum(total * normal, axis=0, keepdims=True).astype(bf16)
    part_ref[rows + 1 : rows + 2, :] = jnp.sum(total, axis=0, keepdims=True).astype(bf16)
    half = part_keep_ref.shape[1]
    side = idx_ref[0] & 1
    part_keep_ref[...] = part_ref[:, pl.ds(pl.multiple_of(side * half, LANES), half)]
    part_send_ref[...] = part_ref[:, pl.ds(pl.multiple_of((1 - side) * half, LANES), half)]
    db_ref[0:1, :] = jnp.sum(gq_ref[...].astype(f32), axis=0, keepdims=True)
    db_ref[1:2, :] = jnp.sum(gv_ref[...].astype(f32), axis=0, keepdims=True)


def pack_kernel(idx_ref, mine_ref, theirs_ref, small_ref, bias_ref, out_ref, line_ref):
    lines, width = line_ref.shape
    local = out_ref.shape[1]
    half = width // 2
    side = idx_ref[0] & 1
    count = small_ref.shape[0]
    line_ref[...] = jnp.zeros_like(line_ref)
    line_ref[0:count, :] = small_ref[...]
    mine = pl.ds(pl.multiple_of(side * half, LANES), half)
    line_ref[count : count + 2, mine] = mine_ref[0:2, :].astype(f32)
    theirs = pl.ds(pl.multiple_of((1 - side) * half, LANES), half)
    line_ref[count : count + 2, theirs] = theirs_ref[0:2, :].astype(f32)
    line_ref[count + 2 : count + 4, 0:local] = bias_ref[...]
    for block in range(width // local):
        out_ref[block * lines : (block + 1) * lines, :] = line_ref[
            :, block * local : (block + 1) * local
        ].astype(bf16)


def first_kernel(idx_ref, tok_ref, gain_ref, mine_ref, theirs_ref, resid_ref, out_ref, grad_ref):
    rows, width = tok_ref.shape
    half = width // 2
    side = idx_ref[0] & 1
    grad_ref[:, pl.ds(pl.multiple_of(side * half, LANES), half)] = mine_ref[...]
    grad_ref[:, pl.ds(pl.multiple_of((1 - side) * half, LANES), half)] = theirs_ref[...]
    normal, rstd = norm_parts(tok_ref[...].astype(f32))
    grad = grad_ref[0:rows, :].astype(f32)
    out_ref[...] = resid_ref[...] + norm_back(grad, normal, rstd, gain_ref[...])


def assemble_kernel(idx_ref, *refs):
    out_ref = refs[-1]
    quarter = out_ref.shape[1] // 4
    for chunk in range(2):
        low = idx_ref[2 + chunk] == 0
        for part in range(3):
            rows = slice(part * quarter, (part + 1) * quarter)
            mine = refs[2 * chunk][rows, :].astype(f32)
            came = refs[2 * chunk + 1][rows, :].astype(f32)
            base = 2 * chunk * quarter
            out_ref[part, base : base + quarter, :] = jnp.where(low, mine, came)
            out_ref[part, base + quarter : base + 2 * quarter, :] = jnp.where(low, came, mine)


def assemble_out_kernel(idx_ref, mine_ref, came_ref, out_ref):
    local = out_ref.shape[0]
    part = local // 2
    low = idx_ref[4] == 0
    for block in range(out_ref.shape[1] // local):
        rows = slice(block * part, (block + 1) * part)
        cols = slice(block * local, (block + 1) * local)
        mine = mine_ref[rows, :].astype(f32)
        came = came_ref[rows, :].astype(f32)
        out_ref[0:part, cols] = jnp.where(low, mine, came)
        out_ref[part:, cols] = jnp.where(low, came, mine)


def on_device(
    tokens,
    gain_attn,
    shift_attn,
    w_qkv,
    b_qv,
    w_out,
    b_out,
    gain_moe,
    shift_moe,
    w_router,
    w_in,
    b_in,
    w_back,
    b_back,
    routes,
    d_out,
):
    groups = lax.axis_size("expert")
    blocks = lax.axis_size("tensor")
    rows, width = tokens.shape
    top = routes.shape[1]
    experts = w_router.shape[1]
    capacity = (top * rows * 16 // (10 * experts) + 7) // 8 * 8
    slots = experts * capacity
    local = w_qkv.shape[2]
    piece = width // blocks
    half = width // 2
    hidden = w_in.shape[2]
    row = lambda vec: vec.reshape(1, -1)
    tensor_id = lax.axis_index("tensor").astype(jnp.int32)
    expert_id = lax.axis_index("expert").astype(jnp.int32)
    chains = [chain_of(groups, masks) for masks in MASKS]
    ids = jnp.stack([tensor_id, expert_id] + [side_of(chain[0][1]) for chain in chains])
    stride = capacity + EXTRA
    row_bits = bits_of(blocks)

    plain, padded, dispatch_place, grad_send = call(
        functools.partial(route_kernel, experts=experts, capacity=capacity),
        [
            sds((rows, slots), bf16),
            sds((rows, experts * stride), bf16),
            sds((slots, rows), bf16),
            sds((slots, piece), bf16),
        ],
        [ids, routes, routes.T, d_out],
        4.4,
        scalars=1,
    )
    w_out_all = gather_tensor(w_out, diagonal=True)
    tokens_in, grad_send = lax.optimization_barrier((tokens, grad_send))
    grad_came = lax.all_to_all(
        grad_send.reshape(experts, capacity, piece), "expert", 0, 0, tiled=True
    ).reshape(slots, piece)

    normed, queries, keys, value_rows, mixed = call(
        attend_kernel,
        [sds((rows, width), bf16)] + [sds((rows, local), bf16)] * 4,
        [tokens_in, row(gain_attn), row(shift_attn), w_qkv, b_qv],
        4.7,
    )
    mixed_all = gather_tensor(mixed)
    residual, second_low, router_probs, send = call(
        functools.partial(middle_kernel, blocks=blocks),
        [
            sds((rows, width), f32),
            sds((rows, width), bf16),
            sds((rows, experts), f32),
            sds((slots, half), bf16),
        ],
        [
            ids,
            *mixed_all,
            *w_out_all,
            tokens,
            row(b_out),
            row(gain_moe),
            row(shift_moe),
            w_router,
            dispatch_place,
        ],
        5.5,
        scalars=1,
        scratch=[pltpu.VMEM((blocks, rows, width), f32)],
    )

    own = lax.all_to_all(
        send.reshape(experts, capacity, half), "expert", 0, 0, tiled=True
    ).reshape(slots, half)
    smem = pl.BlockSpec(memory_space=pltpu.SMEM)
    count = max(1, min(experts, 320 // capacity))
    tile = count * capacity
    steps = slots // tile

    def whole(shape):
        return pl.BlockSpec(shape, lambda i: (0,) * len(shape))

    def by_row(cols):
        return pl.BlockSpec((tile, cols), lambda i: (i, 0))

    grad_rows, unscaled, bias_dot = call(
        functools.partial(early_kernel, blocks=blocks),
        [sds((slots, width), bf16), sds((slots, hidden), f32), sds((slots, 1), f32)],
        [ids, *gather_tensor(grad_came, diagonal=True), w_back[0], b_back],
        7.0,
        grid=(steps,),
        in_specs=[smem] + [by_row(piece)] * blocks + [whole((hidden, width)), whole((1, width))],
        out_specs=[by_row(width), by_row(hidden), by_row(1)],
    )
    own, grad_rows, unscaled = lax.optimization_barrier((own, grad_rows, unscaled))
    other = swap(own, "tensor", 1)

    outs = call(
        functools.partial(expert_kernel, blocks=blocks),
        [sds((experts, stride, piece), bf16)] * blocks
        + [
            sds((slots, hidden), bf16),
            sds((slots, hidden), bf16),
            sds((slots, width), bf16),
            sds((slots, 1), f32),
            sds((1, hidden), f32),
            sds((1, width), f32),
        ],
        [ids, own, other, grad_rows, unscaled, bias_dot, w_in[0], b_in, w_router],
        17.0,
        grid=(steps,),
        in_specs=[
            smem,
            by_row(half),
            by_row(half),
            by_row(width),
            by_row(hidden),
            by_row(1),
            whole((width, hidden)),
            whole((1, hidden)),
            whole((width, experts)),
        ],
        out_specs=[pl.BlockSpec((count, stride, piece), lambda i: (i, 0, 0))] * blocks
        + [
            by_row(hidden),
            by_row(hidden),
            by_row(width),
            by_row(1),
            whole((1, hidden)),
            whole((1, width)),
        ],
    )
    held = scatter_step(dict(enumerate(outs[:blocks])), row_bits[0])
    activated, grad_pre, grad_y, gate, d_b_in, d_b_back = outs[blocks:]
    held, activated, grad_pre, grad_y = lax.optimization_barrier(
        (held, activated, grad_pre, grad_y)
    )

    out_pieces = call(
        back_kernel,
        [sds((slots, piece), bf16)] * blocks,
        [ids, activated, gate, w_back[0], b_back],
        6.5,
        grid=(steps,),
        in_specs=[smem, by_row(hidden), by_row(1), whole((hidden, width)), whole((1, width))],
        out_specs=[by_row(piece)] * blocks,
    )
    kept = [key for key in range(blocks) if not key & 1]
    out_came = [swap(out_pieces[key | 1], "tensor", 1) for key in kept]

    for bit in row_bits[1:]:
        held = scatter_step(held, bit)
    home = lax.all_to_all(held[0], "expert", 0, 0, tiled=True)
    out_sums = call(
        add_pairs_kernel,
        [sds((slots, piece), bf16)] * len(kept),
        [out_pieces[key] for key in kept] + out_came,
        2.0,
        grid=(steps,),
        in_specs=[by_row(piece)] * (2 * len(kept)),
        out_specs=[by_row(piece)] * len(kept),
        after=[held[0]],
    )
    out_held = scatter_sent(dict(zip(kept, out_sums)), row_bits)

    cut = min(256, hidden)
    d_w_back = call(
        outer_kernel,
        [sds((hidden, width), f32)],
        [activated, grad_y],
        7.0,
        grid=(hidden // cut,),
        in_specs=[pl.BlockSpec((slots, cut), lambda i: (0, i)), whole((slots, width))],
        out_specs=[pl.BlockSpec((cut, width), lambda i: (i, 0))],
        after=out_sums,
    )[0][None]
    d_w_in = call(
        outer_halves_kernel,
        [sds((width, hidden), f32)],
        [ids, own, other, grad_pre],
        7.0,
        grid=(4,),
        in_specs=[
            smem,
            pl.BlockSpec((slots, half // 2), lambda i: (0, i % 2)),
            pl.BlockSpec((slots, half // 2), lambda i: (0, i % 2)),
            whole((slots, hidden)),
        ],
        out_specs=[pl.BlockSpec((half // 2, hidden), lambda i: (i, 0))],
        after=out_sums,
    )[0][None]
    dispatch = call(
        combine_kernel,
        [sds((rows, piece), bf16)],
        [padded, home.reshape(experts * stride, piece)],
        1.8,
        after=[d_w_back, d_w_in],
    )[0]
    dispatch_all = gather_tensor(dispatch)
    gate_lines = -(-capacity // piece)
    gate_grads = home[:, capacity : capacity + gate_lines, :].reshape(experts, gate_lines * piece)
    gate_grads = jnp.pad(gate_grads[:, :capacity].astype(f32), ((0, 0), (0, EXTRA)))
    gate_grads = gate_grads.reshape(1, experts * stride)

    out_sent = scatter_last(out_held, row_bits)

    out_home = lax.all_to_all(
        out_sent.reshape(experts, capacity, piece), "expert", 0, 0, tiled=True
    ).reshape(slots, piece)
    mixture = call(
        combine_kernel, [sds((rows, piece), bf16)], [plain, out_home], 1.8    )[0]
    activations = call(
        finish_kernel,
        [sds((rows, width), bf16)],
        [ids, residual, *gather_tensor(mixture)],
        2.6,
        scalars=1,
    )[0]

    grad_resid, out_keep, out_give, grad_mixed, small = call(
        functools.partial(residual_kernel, blocks=blocks, capacity=capacity),
        [
            sds((rows, width), f32),
            sds((half, local), bf16),
            sds((half, local), bf16),
            sds((rows, local), bf16),
            sds((experts + 3, width), f32),
        ],
        [
            ids,
            *dispatch_all,
            gate_grads,
            padded,
            router_probs,
            second_low,
            w_router,
            residual,
            row(gain_moe),
            d_out,
            w_out,
            mixed,
        ],
        6.0,
        scalars=1,
        scratch=[pltpu.VMEM((rows, width), bf16)],
    )
    out_came = swap(out_give, "expert", chains[2][0][0])
    quarter = width // 4
    padded_rows = -(-(rows + 2) // EXTRA) * EXTRA
    outs = call(
        attend_back_kernel,
        [sds((3 * quarter, local), bf16)] * 4
        + [
            sds((2, local), f32),
            sds((padded_rows, half), bf16),
            sds((padded_rows, half), bf16),
            sds((rows, local), bf16),
            sds((rows, local), bf16),
            sds((rows, local), bf16),
        ],
        [ids, queries, keys, value_rows, grad_mixed, normed, w_qkv, tokens],
        8.0,
        scalars=1,
        scratch=[pltpu.VMEM((padded_rows, width), bf16)],
    )
    first_came = swap(outs[1], "expert", chains[0][0][0])
    second_came = swap(outs[3], "expert", chains[1][0][0])
    d_b_qv, part_keep, part_send = outs[4:7]

    mine = add(part_keep, swap(part_send, "tensor", 1))
    part_sum = mine
    for bit in row_bits[1:]:
        mine = add(mine, swap(mine, "tensor", bit))
    theirs = swap(mine, "tensor", 1)
    theirs = swap(mine, "tensor", 1)
    lines = -(-(experts + 7) // EXTRA) * EXTRA
    packed = call(
        pack_kernel,
        [sds((lines * (width // local), local), bf16)],
        [ids, mine[rows:], theirs[rows:], small, d_b_qv],
        1.0,
        scalars=1,
        scratch=[pltpu.VMEM((lines, width), f32)],
    )[0]
    first_sum = call(
        add_kernel, [sds(first_came.shape, bf16)], [outs[0], first_came], 0.8, after=[part_sum]
    )[0]
    first_sums = reduce_experts(first_sum, chains[0])
    second_sums = reduce_experts(add(outs[2], second_came), chains[1])
    out_sum = call(
        add_kernel,
        [sds(out_keep.shape, bf16)],
        [out_keep, out_came],
        0.8,
        after=[second_came],
    )[0]
    out_sums = reduce_experts(out_sum, chains[2])
    *first, packed = spread_experts(first_sums[-1], chains[0], packed)
    second = spread_experts(second_sums[-1], chains[1])[:2]
    d_w_out = spread_experts(out_sums[-1], chains[2])[:2]
    packed = packed.reshape(width // local, lines, local).transpose(1, 0, 2)
    packed = packed.reshape(lines, width).astype(f32)

    d_tokens = call(
        first_kernel,
        [sds((rows, width), f32)],
        [ids, tokens, row(gain_attn), mine, theirs, grad_resid],
        3.9,
        scalars=1,
        scratch=[pltpu.VMEM((padded_rows, width), bf16)],
    )[0]
    d_w_qkv = call(
        assemble_kernel,
        [sds((3, width, local), f32)],
        [ids, *first, *second],
        2.0,
        scalars=1,
        after=[d_tokens],
    )[0]
    d_w_out = call(
        assemble_out_kernel,
        [sds((local, width), f32)],
        [ids, *d_w_out],
        1.0,
        scalars=1,
    )[0]
    return (
        activations,
        d_tokens,
        packed[experts + 3],
        packed[experts + 4],
        d_w_qkv,
        packed[experts + 5 : experts + 7, :local],
        d_w_out,
        packed[experts + 2],
        packed[experts],
        packed[experts + 1],
        packed[:experts].T,
        d_w_in,
        d_b_in,
        d_w_back,
        d_b_back,
    )


def solution(mesh):
    in_specs = (
        P("expert", None),
        P(),
        P(),
        P(None, None, "tensor"),
        P(None, "tensor"),
        P("tensor", None),
        P(),
        P(),
        P(),
        P(),
        P("expert", None, "tensor"),
        P("expert", "tensor"),
        P("expert", "tensor", None),
        P("expert", None),
        P("expert", None),
        P("expert", None),
    )
    out_specs = (
        P("expert", None),
        P("expert", None),
        P(),
        P(),
        P(None, None, "tensor"),
        P(None, "tensor"),
        P("tensor", None),
        P(),
        P(),
        P(),
        P(),
        P("expert", None, "tensor"),
        P("expert", "tensor"),
        P("expert", "tensor", None),
        P("expert", None),
    )
    return jax.shard_map(
        on_device, mesh=mesh, in_specs=in_specs, out_specs=out_specs, check_vma=False
    )
```

```python
import functools

import jax
import jax.numpy as jnp
from jax import lax
from jax.experimental import pallas as pl
from jax.experimental.pallas import tpu as pltpu
from jax.sharding import PartitionSpec as P

HD = 64
SEQ = 197
LANES = 128
VMEM_LIMIT = 52 * 1024 * 1024
EXTRA = 16
MASKS = ((1, 2, 4), (2, 1, 4), (1, 2, 4))
FLOPS_PER_US = 1.15e9

epsilon = 1e-06
f32 = jnp.float32
bf16 = jnp.bfloat16


def dot(left, right, left_dim, right_dim, precision=None):
    return lax.dot_general(
        left,
        right,
        (((left_dim,), (right_dim,)), ((), ())),
        precision=precision,
        preferred_element_type=f32,
    )


def call(
    body, outs, ins, us, grid=None, in_specs=None, out_specs=None, scalars=0, scratch=(), after=()
):
    specs = {"scratch_shapes": list(scratch)}
    if grid is not None:
        specs["grid"] = grid
        specs["out_specs"] = out_specs
    else:
        in_specs = [
            pl.BlockSpec(memory_space=pltpu.SMEM if i < scalars else pltpu.VMEM)
            for i in range(len(ins))
        ]
        specs["out_specs"] = [pl.BlockSpec(memory_space=pltpu.VMEM) for _ in outs]
    specs["in_specs"] = in_specs + [pl.BlockSpec(memory_space=pl.ANY)] * len(after)
    used = len(ins)

    def run(*refs):
        body(*refs[:used], *refs[used + len(after) :])

    return pl.pallas_call(
        run,
        out_shape=outs,
        compiler_params=pltpu.CompilerParams(vmem_limit_bytes=VMEM_LIMIT),
        cost_estimate=pl.CostEstimate(
            flops=int(us * FLOPS_PER_US), bytes_accessed=0, transcendentals=0
        ),
        **specs,
    )(*ins, *after)


def sds(shape, dtype):
    return jax.ShapeDtypeStruct(shape, dtype)


def swap(values, axis, bit):
    count = lax.axis_size(axis)
    return lax.ppermute(values, axis, [(i, i ^ bit) for i in range(count)])


def bits_of(count):
    return [1 << i for i in range(count.bit_length() - 1)]


def gather_tensor(values, diagonal=False):
    count = lax.axis_size("tensor")
    held = {0: values}
    for bit in reversed(bits_of(count)):
        step = bit ^ 1 if diagonal and bit > 1 else bit
        for key in list(held):
            held[key ^ step] = swap(held[key], "tensor", step)
    return [held[key] for key in range(count)]


def add(left, right):
    return (left.astype(f32) + right.astype(f32)).astype(left.dtype)


def scatter_step(held, bit):
    kept = {}
    for key in sorted(held):
        if not key & bit:
            kept[key] = add(held[key], swap(held[key | bit], "tensor", bit))
    return kept


def scatter_sent(held, bits):
    for bit in bits[1:-1]:
        held = scatter_step(held, bit)
    if len(bits) == 1:
        return held
    return {0: held[0], 1: swap(held[bits[-1]], "tensor", bits[-1])}


def scatter_last(held, bits):
    return held[0] if len(bits) == 1 else add(held[0], held[1])


def butterfly(values, axis):
    for bit in bits_of(lax.axis_size(axis)):
        came = swap(values, axis, bit)
        values = add(values, came)
    return values


def chain_of(count, masks):
    masks = [m for m in masks if m < count]
    masks += bits_of(count)[len(masks) :]
    parity = lambda value: bin(value).count("1") % 2
    sides = []
    for step in range(len(masks)):
        wanted = [int(step == other) for other in range(len(masks))]
        fits = [d for d in range(count) if [parity(d & m) for m in masks] == wanted]
        sides.append(fits[0])
    return list(zip(masks, sides))


def side_of(bits):
    index = lax.axis_index("expert")
    total = sum(((index >> b) & 1 for b in range(bits.bit_length()) if (bits >> b) & 1))
    return (total & 1).astype(jnp.int32)


def reduce_experts(values, chain):
    sums = [values]
    for mask, bits in chain[1:]:
        half = values.shape[0] // 2
        side = side_of(bits)
        keep = lax.dynamic_slice_in_dim(values, side * half, half, 0)
        send = lax.dynamic_slice_in_dim(values, (1 - side) * half, half, 0)
        values = add(keep, swap(send, "expert", mask))
        sums.append(values)
    return sums


def spread_experts(values, chain, rider=None):
    count = 0 if rider is None else rider.shape[0]
    for mask, bits in reversed(chain):
        rows = values.shape[0]
        sent = values if rider is None else jnp.concatenate([values, rider], 0)
        came = swap(sent, "expert", mask)
        if rider is not None:
            rider = add(rider, came[rows : rows + count])
        came = came[:rows]
        if (mask, bits) == chain[0]:
            return values, came, rider
        values = jnp.where(
            side_of(bits) == 0,
            jnp.concatenate([values, came], 0),
            jnp.concatenate([came, values], 0),
        )


def norm_parts(values):
    center = values - jnp.mean(values, axis=-1, keepdims=True)
    variance = jnp.mean(center * center, axis=-1, keepdims=True)
    rstd = lax.rsqrt(variance + epsilon)
    return center * rstd, rstd


def norm_back(grad, normal, rstd, gain):
    scaled = grad * gain
    mean_g = jnp.mean(scaled, axis=-1, keepdims=True)
    mean_gn = jnp.mean(scaled * normal, axis=-1, keepdims=True)
    return rstd * (scaled - mean_g - normal * mean_gn)


def same_image(rows):
    left = lax.broadcasted_iota(jnp.int32, (rows, rows), 0)
    right = lax.broadcasted_iota(jnp.int32, (rows, rows), 1)
    left_id = jnp.zeros((rows, rows), jnp.int32)
    right_id = jnp.zeros((rows, rows), jnp.int32)
    for edge in range(SEQ, rows, SEQ):
        left_id = left_id + (left >= edge).astype(jnp.int32)
        right_id = right_id + (right >= edge).astype(jnp.int32)
    return left_id == right_id


def head_probs(queries, keys, inside):
    scores = dot(queries, keys, 1, 1) * (HD ** (-0.5))
    scores = jnp.where(inside, scores, -1e30)
    top = jnp.max(scores, axis=-1, keepdims=True)
    powers = jnp.exp(scores - top)
    return powers * (1.0 / jnp.sum(powers, axis=-1, keepdims=True))


def lane_heads(rows):
    lane = lax.broadcasted_iota(jnp.int32, (rows, LANES), 1)
    return [(lane // HD) == head for head in range(LANES // HD)]


def attend_kernel(tok_ref, gain_ref, shift_ref, w_ref, b_ref, norm_ref, q_ref, k_ref, v_ref, mix_ref):
    rows = tok_ref.shape[0]
    normal, _ = norm_parts(tok_ref[...].astype(f32))
    normed = (normal * gain_ref[...] + shift_ref[...]).astype(bf16)
    norm_ref[...] = normed
    q_ref[...] = (dot(normed, w_ref[0], 1, 0) + b_ref[0:1, :]).astype(bf16)
    k_ref[...] = dot(normed, w_ref[1], 1, 0).astype(bf16)
    v_ref[...] = (dot(normed, w_ref[2], 1, 0) + b_ref[1:2, :]).astype(bf16)
    inside = same_image(rows)
    heads = lane_heads(rows)
    for start in range(0, q_ref.shape[1], LANES):
        cols = slice(start, start + LANES)
        queries, keys, value_rows = q_ref[:, cols], k_ref[:, cols], v_ref[:, cols]
        mixed = jnp.zeros((rows, LANES), f32)
        for mask in heads:
            probs = head_probs(jnp.where(mask, queries, 0).astype(bf16), keys, inside)
            mixed = jnp.where(mask, dot(probs.astype(bf16), value_rows, 1, 0), mixed)
        mix_ref[:, cols] = mixed.astype(bf16)


def slot_numbers(named, earlier, ids, axis, stride):
    numbers = []
    for mask in named:
        slot = jnp.sum(jnp.where(mask, earlier, 0.0), axis=axis, keepdims=True).astype(jnp.int32)
        owner = jnp.sum(jnp.where(mask, ids, 0), axis=axis, keepdims=True)
        numbers.append(owner * stride + slot)
    return numbers


def one_hot(targets, shape, axis):
    ids = lax.broadcasted_iota(jnp.int32, shape, axis)
    table = jnp.zeros(shape, f32)
    for target in targets:
        table = jnp.where(ids == target, 1.0, table)
    return table.astype(bf16)


def route_kernel(
    idx_ref,
    routes_ref,
    flipped_ref,
    dout_ref,
    plain_ref,
    padded_ref,
    dispatch_ref,
    send_ref,
    *,
    experts,
    capacity,
):
    place_kernel(routes_ref, plain_ref, padded_ref, experts=experts, capacity=capacity)
    rows = dispatch_ref.shape[1]
    width = send_ref.shape[1]
    first = lax.broadcasted_iota(jnp.int32, (rows, rows), 0)
    second = lax.broadcasted_iota(jnp.int32, (rows, rows), 1)
    ids = lax.broadcasted_iota(jnp.int32, (experts, rows), 0)
    named = [flipped_ref[k : k + 1, :] == ids for k in range(flipped_ref.shape[0])]
    tally = sum(m.astype(f32) for m in named).astype(bf16)
    earlier = dot(tally, (first < second).astype(f32).astype(bf16), 1, 0)
    numbers = slot_numbers(named, earlier, ids, 0, capacity)
    dispatch_ref[...] = one_hot(numbers, dispatch_ref.shape, 0)
    start = pl.multiple_of(idx_ref[0] * width, LANES)
    send_ref[...] = dot(dispatch_ref[...], dout_ref[:, pl.ds(start, width)], 1, 0).astype(bf16)


def place_kernel(routes_ref, plain_ref, padded_ref, *, experts, capacity):
    rows = plain_ref.shape[0]
    first = lax.broadcasted_iota(jnp.int32, (rows, rows), 0)
    second = lax.broadcasted_iota(jnp.int32, (rows, rows), 1)
    ids = lax.broadcasted_iota(jnp.int32, (rows, experts), 1)
    named = [routes_ref[:, k : k + 1] == ids for k in range(routes_ref.shape[1])]
    tally = sum(m.astype(f32) for m in named).astype(bf16)
    earlier = dot((second < first).astype(f32).astype(bf16), tally, 1, 0)
    for ref, stride in ((plain_ref, capacity), (padded_ref, capacity + EXTRA)):
        ref[...] = one_hot(slot_numbers(named, earlier, ids, 1, stride), ref.shape, 1)


def middle_kernel(*refs, blocks):
    idx_ref, refs = refs[0], refs[1:]
    mix_refs, w_refs, refs = refs[:blocks], refs[blocks : 2 * blocks], refs[2 * blocks :]
    tok_ref, bias_ref, gain_ref, shift_ref, router_ref, dispatch_ref = refs[:6]
    resid_ref, second_ref, probs_ref, send_ref, terms_ref = refs[6:]
    width = send_ref.shape[1]
    for key in range(blocks):
        terms_ref[key] = dot(mix_refs[key][...], w_refs[key][...], 1, 0)
    terms = [terms_ref[key] for key in range(blocks)]
    while len(terms) > 1:
        terms = [terms[i] + terms[i + 1] for i in range(0, len(terms), 2)]
    residual = tok_ref[...].astype(f32) + terms[0] + bias_ref[...]
    resid_ref[...] = residual
    normal, _ = norm_parts(residual)
    second_ref[...] = (normal * gain_ref[...] + shift_ref[...]).astype(bf16)
    start = pl.multiple_of((idx_ref[0] & 1) * width, LANES)
    send_ref[...] = dot(dispatch_ref[...], second_ref[:, pl.ds(start, width)], 1, 0).astype(bf16)
    logits = dot(second_ref[...], router_ref[...], 1, 0)
    powers = jnp.exp(logits - jnp.max(logits, axis=-1, keepdims=True))
    probs_ref[...] = powers / jnp.sum(powers, axis=-1, keepdims=True)


def early_kernel(*refs, blocks):
    idx_ref, piece_refs = refs[0], refs[1 : 1 + blocks]
    w_ref, bias_ref, rows_ref, unscaled_ref, bias_dot_ref = refs[1 + blocks :]
    piece = piece_refs[0].shape[-1]
    for key, piece_ref in enumerate(piece_refs):
        cols = pl.ds(pl.multiple_of((idx_ref[0] ^ key) * piece, LANES), piece)
        rows_ref[:, cols] = piece_ref[...]
    unscaled_ref[...] = dot(rows_ref[...], w_ref[...], 1, 1)
    bias_dot_ref[...] = jnp.sum(
        rows_ref[...].astype(f32) * bias_ref[...], axis=1, keepdims=True
    ) * (1.0 / blocks)


def expert_kernel(
    idx_ref,
    own_ref,
    other_ref,
    grad_ref,
    unscaled_ref,
    bias_dot_ref,
    w_in_ref,
    b_in_ref,
    router_ref,
    *outs,
    blocks,
):
    piece_refs = outs[:blocks]
    act_ref, pre_ref, grady_ref, gate_ref, dbin_ref, dbback_ref = outs[blocks:]
    count, capacity = piece_refs[0].shape[0], piece_refs[0].shape[1] - EXTRA
    tensor_id, expert_id = idx_ref[0], idx_ref[1]
    side = tensor_id & 1
    width = w_in_ref.shape[0] // 2
    piece = w_in_ref.shape[0] // blocks
    own, other = own_ref[...], other_ref[...]
    low_half = jnp.where(side == 0, own, other)
    high_half = jnp.where(side == 0, other, own)
    logits = dot(low_half, router_ref[0:width, :], 1, 0) + dot(
        high_half, router_ref[width:, :], 1, 0
    )
    powers = jnp.exp(logits - jnp.max(logits, axis=-1, keepdims=True))
    ids = lax.broadcasted_iota(jnp.int32, logits.shape, 1)
    gate = jnp.sum(jnp.where(ids == expert_id, powers, 0.0), axis=-1, keepdims=True) / jnp.sum(
        powers, axis=-1, keepdims=True
    )
    gate_ref[...] = gate
    pre_act = (
        dot(low_half, w_in_ref[0:width, :], 1, 0)
        + dot(high_half, w_in_ref[width:, :], 1, 0)
        + b_in_ref[...]
    )
    cdf = 0.5 * (1.0 + lax.erf(pre_act * (2.0**-0.5)))
    density = jnp.exp(-0.5 * pre_act * pre_act) * 0.3989422804014327
    act = (pre_act * cdf).astype(bf16)
    act_ref[...] = act
    unscaled = unscaled_ref[...]
    grad_pre = (gate * unscaled * (cdf + pre_act * density)).astype(bf16)
    pre_ref[...] = grad_pre
    grad_rows = grad_ref[...].astype(f32)
    gate_grads = jnp.sum(act.astype(f32) * unscaled, axis=1, keepdims=True) + bias_dot_ref[...]
    gate_grads = jnp.broadcast_to(gate_grads, (gate_grads.shape[0], LANES)).T
    grad_y = (gate * grad_rows).astype(bf16)
    grady_ref[...] = grad_y

    @pl.when(pl.program_id(0) == 0)
    def _():
        dbin_ref[...] = jnp.zeros_like(dbin_ref)
        dbback_ref[...] = jnp.zeros_like(dbback_ref)

    ones = jnp.ones((8, grad_pre.shape[0]), bf16)
    dbin_ref[...] += dot(ones, grad_pre, 1, 0)[0:1, :]
    dbback_ref[...] += dot(ones, grad_y, 1, 0)[0:1, :]
    for key, piece_ref in enumerate(piece_refs):
        start = pl.multiple_of((tensor_id ^ key) * piece, LANES)
        rows = dot(grad_pre, w_in_ref[pl.ds(start, piece), :], 1, 1)
        for source in range(count):
            part = slice(source * capacity, (source + 1) * capacity)
            piece_ref[source, 0:capacity, :] = rows[part, :].astype(bf16)
            piece_ref[source, capacity : capacity + EXTRA, :] = jnp.zeros((EXTRA, piece), bf16)
            for first in range(0, capacity, piece):
                lanes = min(piece, capacity - first)
                place = capacity + first // piece
                here = source * capacity + first
                piece_ref[source, place : place + 1, 0:lanes] = gate_grads[
                    0:1, here : here + lanes
                ].astype(bf16)


def back_kernel(idx_ref, act_ref, gate_ref, w_ref, bias_ref, *piece_refs):
    blocks = len(piece_refs)
    piece = piece_refs[0].shape[-1]
    for key, piece_ref in enumerate(piece_refs):
        cols = pl.ds(pl.multiple_of((idx_ref[0] ^ key) * piece, LANES), piece)
        rows = dot(act_ref[...], w_ref[:, cols], 1, 0) + bias_ref[:, cols] * (1.0 / blocks)
        piece_ref[...] = (gate_ref[...] * rows).astype(bf16)


def outer_kernel(left_ref, right_ref, out_ref):
    out_ref[...] = dot(left_ref[...], right_ref[...], 0, 0)


def outer_halves_kernel(idx_ref, own_ref, other_ref, right_ref, out_ref):
    mine = (idx_ref[0] & 1) == pl.program_id(0) // 2

    @pl.when(mine)
    def _():
        out_ref[...] = dot(own_ref[...], right_ref[...], 0, 0)

    @pl.when(jnp.logical_not(mine))
    def _():
        out_ref[...] = dot(other_ref[...], right_ref[...], 0, 0)


def add_pairs_kernel(*refs):
    count = len(refs) // 3
    for left_ref, right_ref, out_ref in zip(refs[:count], refs[count : 2 * count], refs[2 * count :]):
        out_ref[...] = (left_ref[...].astype(f32) + right_ref[...].astype(f32)).astype(bf16)


def add_kernel(left_ref, right_ref, out_ref):
    out_ref[...] = (left_ref[...].astype(f32) + right_ref[...].astype(f32)).astype(bf16)


def combine_kernel(place_ref, home_ref, out_ref):
    out_ref[...] = dot(place_ref[...], home_ref[...], 1, 0).astype(bf16)


def finish_kernel(idx_ref, resid_ref, *refs):
    piece_refs, out_ref = refs[:-1], refs[-1]
    piece = piece_refs[0].shape[1]
    for key, piece_ref in enumerate(piece_refs):
        cols = pl.ds(pl.multiple_of((idx_ref[0] ^ key) * piece, LANES), piece)
        out_ref[:, cols] = (resid_ref[:, cols] + piece_ref[...].astype(f32)).astype(bf16)


def residual_kernel(*refs, blocks, capacity):
    idx_ref, piece_refs, refs = refs[0], refs[1 : 1 + blocks], refs[1 + blocks :]
    residual_body(idx_ref, piece_refs, *refs, capacity=capacity)


def residual_body(
    idx_ref,
    piece_refs,
    gg_ref,
    place_ref,
    probs_ref,
    second_ref,
    router_ref,
    resid_ref,
    gain_ref,
    dout_ref,
    w_ref,
    mix_ref,
    grad_ref,
    dw_keep_ref,
    dw_send_ref,
    gmix_ref,
    small_ref,
    disp_ref,
    *,
    capacity,
):
    probs = probs_ref[...]
    experts = probs.shape[1]
    slots = place_ref.shape[1]
    piece = piece_refs[0].shape[1]
    stride = capacity + EXTRA
    lane = lax.broadcasted_iota(jnp.int32, (experts, slots), 1)
    first = lax.broadcasted_iota(jnp.int32, (experts, slots), 0) * stride
    segment = (lane >= first) & (lane < first + capacity)
    gate_rows = jnp.where(segment, jnp.broadcast_to(gg_ref[...], (experts, slots)), 0.0)
    grad_probs = dot(place_ref[...], gate_rows.astype(bf16), 1, 1)
    for key, piece_ref in enumerate(piece_refs):
        cols = pl.ds(pl.multiple_of((idx_ref[0] ^ key) * piece, LANES), piece)
        disp_ref[:, cols] = piece_ref[...]
    grad_logits = (
        probs * (grad_probs - jnp.sum(probs * grad_probs, axis=1, keepdims=True))
    ).astype(bf16)
    second_grad = disp_ref[...].astype(f32) + dot(grad_logits, router_ref[...], 1, 1)
    normal, rstd = norm_parts(resid_ref[...])
    grad_resid = dout_ref[...].astype(f32) + norm_back(second_grad, normal, rstd, gain_ref[...])
    grad_ref[...] = grad_resid
    branch = grad_resid.astype(bf16)
    gmix_ref[...] = dot(branch, w_ref[...], 1, 1).astype(bf16)
    local = dw_keep_ref.shape[1]
    part = local // 2
    for ref, side in ((dw_keep_ref, idx_ref[4]), (dw_send_ref, 1 - idx_ref[4])):
        if part % LANES == 0:
            left = mix_ref[:, pl.ds(pl.multiple_of(side * part, LANES), part)]
        else:
            left = jnp.where(side == 0, mix_ref[:, 0:part], mix_ref[:, part:])
        product = dot(left, branch, 0, 0).astype(bf16)
        for block in range(product.shape[1] // local):
            ref[block * part : (block + 1) * part, :] = product[
                :, block * local : (block + 1) * local
            ]
    small_ref[0:experts, :] = dot(grad_logits, second_ref[...], 0, 0)
    small_ref[experts : experts + 1, :] = jnp.sum(second_grad * normal, axis=0, keepdims=True)
    small_ref[experts + 1 : experts + 2, :] = jnp.sum(second_grad, axis=0, keepdims=True)
    small_ref[experts + 2 : experts + 3, :] = jnp.sum(grad_resid, axis=0, keepdims=True)


def attend_back_kernel(
    idx_ref,
    q_ref,
    k_ref,
    v_ref,
    gmix_ref,
    norm_ref,
    w_ref,
    tok_ref,
    first_keep_ref,
    first_send_ref,
    second_keep_ref,
    second_send_ref,
    db_ref,
    part_keep_ref,
    part_send_ref,
    gq_ref,
    gk_ref,
    gv_ref,
    part_ref,
):
    rows = q_ref.shape[0]
    inside = same_image(rows)
    heads = lane_heads(rows)
    scale = HD ** (-0.5)
    for start in range(0, q_ref.shape[1], LANES):
        cols = slice(start, start + LANES)
        queries, keys, value_rows = q_ref[:, cols], k_ref[:, cols], v_ref[:, cols]
        grad_mixed = gmix_ref[:, cols]
        grad_q = jnp.zeros((rows, LANES), f32)
        grad_k = jnp.zeros((rows, LANES), f32)
        grad_v = jnp.zeros((rows, LANES), f32)
        for mask in heads:
            one_q = jnp.where(mask, queries, 0).astype(bf16)
            one_g = jnp.where(mask, grad_mixed, 0).astype(bf16)
            probs = head_probs(one_q, keys, inside)
            grad_v = grad_v + dot(probs.astype(bf16), one_g, 0, 0)
            grad_attn = dot(one_g, value_rows, 1, 1)
            delta = jnp.sum(probs * grad_attn, axis=-1, keepdims=True)
            grad_scores = (probs * (grad_attn - delta)).astype(bf16)
            grad_q = jnp.where(mask, dot(grad_scores, keys, 1, 0), grad_q)
            grad_k = grad_k + dot(grad_scores, one_q, 0, 0)
        gq_ref[:, cols] = (grad_q * scale).astype(bf16)
        gk_ref[:, cols] = (grad_k * scale).astype(bf16)
        gv_ref[:, cols] = grad_v.astype(bf16)
    quarter = norm_ref.shape[1] // 4
    total = None
    for part, ref in enumerate((gq_ref, gk_ref, gv_ref)):
        grads = ref[...]
        here = slice(part * quarter, (part + 1) * quarter)
        for side, base, keep_ref, send_ref in (
            (idx_ref[2], 0, first_keep_ref, first_send_ref),
            (idx_ref[3], 2, second_keep_ref, second_send_ref),
        ):
            for target, block in ((keep_ref, base + side), (send_ref, base + 1 - side)):
                cols = pl.ds(pl.multiple_of(block * quarter, LANES), quarter)
                target[here, :] = dot(norm_ref[:, cols], grads, 0, 0).astype(bf16)
        term = dot(grads, w_ref[part], 1, 1)
        total = term if total is None else total + term
    normal, _ = norm_parts(tok_ref[...].astype(f32))
    part_ref[0:rows, :] = total.astype(bf16)
    part_ref[rows:, :] = jnp.zeros((part_ref.shape[0] - rows, total.shape[1]), bf16)
    part_ref[rows : rows + 1, :] = jnp.sum(total * normal, axis=0, keepdims=True).astype(bf16)
    part_ref[rows + 1 : rows + 2, :] = jnp.sum(total, axis=0, keepdims=True).astype(bf16)
    half = part_keep_ref.shape[1]
    side = idx_ref[0] & 1
    part_keep_ref[...] = part_ref[:, pl.ds(pl.multiple_of(side * half, LANES), half)]
    part_send_ref[...] = part_ref[:, pl.ds(pl.multiple_of((1 - side) * half, LANES), half)]
    db_ref[0:1, :] = jnp.sum(gq_ref[...].astype(f32), axis=0, keepdims=True)
    db_ref[1:2, :] = jnp.sum(gv_ref[...].astype(f32), axis=0, keepdims=True)


def pack_kernel(idx_ref, mine_ref, theirs_ref, small_ref, bias_ref, out_ref, line_ref):
    lines, width = line_ref.shape
    local = out_ref.shape[1]
    half = width // 2
    side = idx_ref[0] & 1
    count = small_ref.shape[0]
    line_ref[...] = jnp.zeros_like(line_ref)
    line_ref[0:count, :] = small_ref[...]
    mine = pl.ds(pl.multiple_of(side * half, LANES), half)
    line_ref[count : count + 2, mine] = mine_ref[0:2, :].astype(f32)
    theirs = pl.ds(pl.multiple_of((1 - side) * half, LANES), half)
    line_ref[count : count + 2, theirs] = theirs_ref[0:2, :].astype(f32)
    line_ref[count + 2 : count + 4, 0:local] = bias_ref[...]
    for block in range(width // local):
        out_ref[block * lines : (block + 1) * lines, :] = line_ref[
            :, block * local : (block + 1) * local
        ].astype(bf16)


def first_kernel(idx_ref, tok_ref, gain_ref, mine_ref, theirs_ref, resid_ref, out_ref, grad_ref):
    rows, width = tok_ref.shape
    half = width // 2
    side = idx_ref[0] & 1
    grad_ref[:, pl.ds(pl.multiple_of(side * half, LANES), half)] = mine_ref[...]
    grad_ref[:, pl.ds(pl.multiple_of((1 - side) * half, LANES), half)] = theirs_ref[...]
    normal, rstd = norm_parts(tok_ref[...].astype(f32))
    grad = grad_ref[0:rows, :].astype(f32)
    out_ref[...] = resid_ref[...] + norm_back(grad, normal, rstd, gain_ref[...])


def assemble_kernel(idx_ref, *refs):
    out_ref = refs[-1]
    quarter = out_ref.shape[1] // 4
    for chunk in range(2):
        low = idx_ref[2 + chunk] == 0
        for part in range(3):
            rows = slice(part * quarter, (part + 1) * quarter)
            mine = refs[2 * chunk][rows, :].astype(f32)
            came = refs[2 * chunk + 1][rows, :].astype(f32)
            base = 2 * chunk * quarter
            out_ref[part, base : base + quarter, :] = jnp.where(low, mine, came)
            out_ref[part, base + quarter : base + 2 * quarter, :] = jnp.where(low, came, mine)


def assemble_out_kernel(idx_ref, mine_ref, came_ref, out_ref):
    local = out_ref.shape[0]
    part = local // 2
    low = idx_ref[4] == 0
    for block in range(out_ref.shape[1] // local):
        rows = slice(block * part, (block + 1) * part)
        cols = slice(block * local, (block + 1) * local)
        mine = mine_ref[rows, :].astype(f32)
        came = came_ref[rows, :].astype(f32)
        out_ref[0:part, cols] = jnp.where(low, mine, came)
        out_ref[part:, cols] = jnp.where(low, came, mine)


def on_device(
    tokens,
    gain_attn,
    shift_attn,
    w_qkv,
    b_qv,
    w_out,
    b_out,
    gain_moe,
    shift_moe,
    w_router,
    w_in,
    b_in,
    w_back,
    b_back,
    routes,
    d_out,
):
    groups = lax.axis_size("expert")
    blocks = lax.axis_size("tensor")
    rows, width = tokens.shape
    top = routes.shape[1]
    experts = w_router.shape[1]
    capacity = (top * rows * 16 // (10 * experts) + 7) // 8 * 8
    slots = experts * capacity
    local = w_qkv.shape[2]
    piece = width // blocks
    half = width // 2
    hidden = w_in.shape[2]
    row = lambda vec: vec.reshape(1, -1)
    tensor_id = lax.axis_index("tensor").astype(jnp.int32)
    expert_id = lax.axis_index("expert").astype(jnp.int32)
    chains = [chain_of(groups, masks) for masks in MASKS]
    ids = jnp.stack([tensor_id, expert_id] + [side_of(chain[0][1]) for chain in chains])
    stride = capacity + EXTRA
    row_bits = bits_of(blocks)

    plain, padded, dispatch_place, grad_send = call(
        functools.partial(route_kernel, experts=experts, capacity=capacity),
        [
            sds((rows, slots), bf16),
            sds((rows, experts * stride), bf16),
            sds((slots, rows), bf16),
            sds((slots, piece), bf16),
        ],
        [ids, routes, routes.T, d_out],
        4.4,
        scalars=1,
    )
    w_out_all = gather_tensor(w_out, diagonal=True)
    tokens_in, grad_send = lax.optimization_barrier((tokens, grad_send))
    grad_came = lax.all_to_all(
        grad_send.reshape(experts, capacity, piece), "expert", 0, 0, tiled=True
    ).reshape(slots, piece)

    normed, queries, keys, value_rows, mixed = call(
        attend_kernel,
        [sds((rows, width), bf16)] + [sds((rows, local), bf16)] * 4,
        [tokens_in, row(gain_attn), row(shift_attn), w_qkv, b_qv],
        4.7,
    )
    mixed_all = gather_tensor(mixed)
    residual, second_low, router_probs, send = call(
        functools.partial(middle_kernel, blocks=blocks),
        [
            sds((rows, width), f32),
            sds((rows, width), bf16),
            sds((rows, experts), f32),
            sds((slots, half), bf16),
        ],
        [
            ids,
            *mixed_all,
            *w_out_all,
            tokens,
            row(b_out),
            row(gain_moe),
            row(shift_moe),
            w_router,
            dispatch_place,
        ],
        5.5,
        scalars=1,
        scratch=[pltpu.VMEM((blocks, rows, width), f32)],
    )

    own = lax.all_to_all(
        send.reshape(experts, capacity, half), "expert", 0, 0, tiled=True
    ).reshape(slots, half)
    smem = pl.BlockSpec(memory_space=pltpu.SMEM)
    count = max(1, min(experts, 320 // capacity))
    tile = count * capacity
    steps = slots // tile

    def whole(shape):
        return pl.BlockSpec(shape, lambda i: (0,) * len(shape))

    def by_row(cols):
        return pl.BlockSpec((tile, cols), lambda i: (i, 0))

    grad_rows, unscaled, bias_dot = call(
        functools.partial(early_kernel, blocks=blocks),
        [sds((slots, width), bf16), sds((slots, hidden), f32), sds((slots, 1), f32)],
        [ids, *gather_tensor(grad_came, diagonal=True), w_back[0], b_back],
        7.0,
        grid=(steps,),
        in_specs=[smem] + [by_row(piece)] * blocks + [whole((hidden, width)), whole((1, width))],
        out_specs=[by_row(width), by_row(hidden), by_row(1)],
    )
    own, grad_rows, unscaled = lax.optimization_barrier((own, grad_rows, unscaled))
    other = swap(own, "tensor", 1)

    outs = call(
        functools.partial(expert_kernel, blocks=blocks),
        [sds((experts, stride, piece), bf16)] * blocks
        + [
            sds((slots, hidden), bf16),
            sds((slots, hidden), bf16),
            sds((slots, width), bf16),
            sds((slots, 1), f32),
            sds((1, hidden), f32),
            sds((1, width), f32),
        ],
        [ids, own, other, grad_rows, unscaled, bias_dot, w_in[0], b_in, w_router],
        17.0,
        grid=(steps,),
        in_specs=[
            smem,
            by_row(half),
            by_row(half),
            by_row(width),
            by_row(hidden),
            by_row(1),
            whole((width, hidden)),
            whole((1, hidden)),
            whole((width, experts)),
        ],
        out_specs=[pl.BlockSpec((count, stride, piece), lambda i: (i, 0, 0))] * blocks
        + [
            by_row(hidden),
            by_row(hidden),
            by_row(width),
            by_row(1),
            whole((1, hidden)),
            whole((1, width)),
        ],
    )
    held = scatter_step(dict(enumerate(outs[:blocks])), row_bits[0])
    activated, grad_pre, grad_y, gate, d_b_in, d_b_back = outs[blocks:]
    held, activated, grad_pre, grad_y = lax.optimization_barrier(
        (held, activated, grad_pre, grad_y)
    )

    out_pieces = call(
        back_kernel,
        [sds((slots, piece), bf16)] * blocks,
        [ids, activated, gate, w_back[0], b_back],
        6.5,
        grid=(steps,),
        in_specs=[smem, by_row(hidden), by_row(1), whole((hidden, width)), whole((1, width))],
        out_specs=[by_row(piece)] * blocks,
    )
    kept = [key for key in range(blocks) if not key & 1]
    out_came = [swap(out_pieces[key | 1], "tensor", 1) for key in kept]

    for bit in row_bits[1:]:
        held = scatter_step(held, bit)
    home = lax.all_to_all(held[0], "expert", 0, 0, tiled=True)
    out_sums = call(
        add_pairs_kernel,
        [sds((slots, piece), bf16)] * len(kept),
        [out_pieces[key] for key in kept] + out_came,
        2.0,
        grid=(steps,),
        in_specs=[by_row(piece)] * (2 * len(kept)),
        out_specs=[by_row(piece)] * len(kept),
        after=[held[0]],
    )
    out_held = scatter_sent(dict(zip(kept, out_sums)), row_bits)

    cut = min(256, hidden)
    d_w_back = call(
        outer_kernel,
        [sds((hidden, width), f32)],
        [activated, grad_y],
        7.0,
        grid=(hidden // cut,),
        in_specs=[pl.BlockSpec((slots, cut), lambda i: (0, i)), whole((slots, width))],
        out_specs=[pl.BlockSpec((cut, width), lambda i: (i, 0))],
        after=out_sums,
    )[0][None]
    d_w_in = call(
        outer_halves_kernel,
        [sds((width, hidden), f32)],
        [ids, own, other, grad_pre],
        7.0,
        grid=(4,),
        in_specs=[
            smem,
            pl.BlockSpec((slots, half // 2), lambda i: (0, i % 2)),
            pl.BlockSpec((slots, half // 2), lambda i: (0, i % 2)),
            whole((slots, hidden)),
        ],
        out_specs=[pl.BlockSpec((half // 2, hidden), lambda i: (i, 0))],
        after=out_sums,
    )[0][None]
    dispatch = call(
        combine_kernel,
        [sds((rows, piece), bf16)],
        [padded, home.reshape(experts * stride, piece)],
        1.8,
        after=[d_w_back, d_w_in],
    )[0]
    dispatch_all = gather_tensor(dispatch)
    gate_lines = -(-capacity // piece)
    gate_grads = home[:, capacity : capacity + gate_lines, :].reshape(experts, gate_lines * piece)
    gate_grads = jnp.pad(gate_grads[:, :capacity].astype(f32), ((0, 0), (0, EXTRA)))
    gate_grads = gate_grads.reshape(1, experts * stride)

    out_sent = scatter_last(out_held, row_bits)

    out_home = lax.all_to_all(
        out_sent.reshape(experts, capacity, piece), "expert", 0, 0, tiled=True
    ).reshape(slots, piece)
    mixture = call(
        combine_kernel, [sds((rows, piece), bf16)], [plain, out_home], 1.8    )[0]
    activations = call(
        finish_kernel,
        [sds((rows, width), bf16)],
        [ids, residual, *gather_tensor(mixture)],
        2.6,
        scalars=1,
    )[0]

    grad_resid, out_keep, out_give, grad_mixed, small = call(
        functools.partial(residual_kernel, blocks=blocks, capacity=capacity),
        [
            sds((rows, width), f32),
            sds((half, local), bf16),
            sds((half, local), bf16),
            sds((rows, local), bf16),
            sds((experts + 3, width), f32),
        ],
        [
            ids,
            *dispatch_all,
            gate_grads,
            padded,
            router_probs,
            second_low,
            w_router,
            residual,
            row(gain_moe),
            d_out,
            w_out,
            mixed,
        ],
        6.0,
        scalars=1,
        scratch=[pltpu.VMEM((rows, width), bf16)],
    )
    out_came = swap(out_give, "expert", chains[2][0][0])
    quarter = width // 4
    padded_rows = -(-(rows + 2) // EXTRA) * EXTRA
    outs = call(
        attend_back_kernel,
        [sds((3 * quarter, local), bf16)] * 4
        + [
            sds((2, local), f32),
            sds((padded_rows, half), bf16),
            sds((padded_rows, half), bf16),
            sds((rows, local), bf16),
            sds((rows, local), bf16),
            sds((rows, local), bf16),
        ],
        [ids, queries, keys, value_rows, grad_mixed, normed, w_qkv, tokens],
        8.0,
        scalars=1,
        scratch=[pltpu.VMEM((padded_rows, width), bf16)],
    )
    first_came = swap(outs[1], "expert", chains[0][0][0])
    second_came = swap(outs[3], "expert", chains[1][0][0])
    d_b_qv, part_keep, part_send = outs[4:7]

    mine = add(part_keep, swap(part_send, "tensor", 1))
    part_sum = mine
    for bit in row_bits[1:]:
        mine = add(mine, swap(mine, "tensor", bit))
    theirs = swap(mine, "tensor", 1)
    theirs = swap(mine, "tensor", 1)
    lines = -(-(experts + 7) // EXTRA) * EXTRA
    packed = call(
        pack_kernel,
        [sds((lines * (width // local), local), bf16)],
        [ids, mine[rows:], theirs[rows:], small, d_b_qv],
        1.0,
        scalars=1,
        scratch=[pltpu.VMEM((lines, width), f32)],
    )[0]
    first_sum = call(
        add_kernel, [sds(first_came.shape, bf16)], [outs[0], first_came], 0.8, after=[part_sum]
    )[0]
    first_sums = reduce_experts(first_sum, chains[0])
    second_sums = reduce_experts(add(outs[2], second_came), chains[1])
    out_sum = call(
        add_kernel,
        [sds(out_keep.shape, bf16)],
        [out_keep, out_came],
        0.8,
        after=[second_came],
    )[0]
    out_sums = reduce_experts(out_sum, chains[2])
    *first, packed = spread_experts(first_sums[-1], chains[0], packed)
    second = spread_experts(second_sums[-1], chains[1])[:2]
    d_w_out = spread_experts(out_sums[-1], chains[2])[:2]
    packed = packed.reshape(width // local, lines, local).transpose(1, 0, 2)
    packed = packed.reshape(lines, width).astype(f32)

    d_tokens = call(
        first_kernel,
        [sds((rows, width), f32)],
        [ids, tokens, row(gain_attn), mine, theirs, grad_resid],
        3.9,
        scalars=1,
        scratch=[pltpu.VMEM((padded_rows, width), bf16)],
    )[0]
    d_w_qkv = call(
        assemble_kernel,
        [sds((3, width, local), f32)],
        [ids, *first, *second],
        2.0,
        scalars=1,
        after=[d_tokens],
    )[0]
    d_w_out = call(
        assemble_out_kernel,
        [sds((local, width), f32)],
        [ids, *d_w_out],
        1.0,
        scalars=1,
    )[0]
    return (
        activations,
        d_tokens,
        packed[experts + 3],
        packed[experts + 4],
        d_w_qkv,
        packed[experts + 5 : experts + 7, :local],
        d_w_out,
        packed[experts + 2],
        packed[experts],
        packed[experts + 1],
        packed[:experts].T,
        d_w_in,
        d_b_in,
        d_w_back,
        d_b_back,
    )


def solution(mesh):
    in_specs = (
        P("expert", None),
        P(),
        P(),
        P(None, None, "tensor"),
        P(None, "tensor"),
        P("tensor", None),
        P(),
        P(),
        P(),
        P(),
        P("expert", None, "tensor"),
        P("expert", "tensor"),
        P("expert", "tensor", None),
        P("expert", None),
        P("expert", None),
        P("expert", None),
    )
    out_specs = (
        P("expert", None),
        P("expert", None),
        P(),
        P(),
        P(None, None, "tensor"),
        P(None, "tensor"),
        P("tensor", None),
        P(),
        P(),
        P(),
        P(),
        P("expert", None, "tensor"),
        P("expert", "tensor"),
        P("expert", "tensor", None),
        P("expert", None),
    )
    return jax.shard_map(
        on_device, mesh=mesh, in_specs=in_specs, out_specs=out_specs, check_vma=False
    )
```
